512 devices in a mesh: bx: 16 (over x_lo, y, core), by: 32 (over z, x_hi).
Axes of the slice: x: 4 (x_hi: 2, x_lo: 2; x = x_hi * 2 + x_lo), y: 4, z: 16, core: 2. Of those that a mesh axis runs over, the one named last changes fastest.
Arguments:
- solution: float32 [4, 2048, 2048], P(None, 'by', 'bx'), may hold values from -6 to 6
- source: float32 [4, 2048, 2048], P(None, 'by', 'bx'), may hold values from -12 to 12
- class_ids: int32 [4, 2048, 2048], P(None, 'by', 'bx'), may hold values from 0 to 7
- conductivity: float32 [8], replicated, may hold values from 0.3 to 3
- spacing_x: float32 [2048], P('bx'), may hold values from 0.7 to 1.4
- spacing_y: float32 [2048], P('by'), may hold values from 0.7 to 1.4
- spacing_z: float32 [4], replicated, may hold values from 0.7 to 1.4
- forward_x: bfloat16 [2048, 2048], P('bx'), may hold values from -0.125 to 0.125
- forward_y: bfloat16 [2048, 2048], P('by'), may hold values from -0.125 to 0.125
- forward_z: bfloat16 [4, 4], replicated, may hold values from -3 to 3
- inverse_x: bfloat16 [2048, 2048], P('bx'), may hold values from -0.125 to 0.125
- inverse_y: bfloat16 [2048, 2048], P('by'), may hold values from -0.125 to 0.125
- inverse_z: bfloat16 [4, 4], replicated, may hold values from -3 to 3
- eigen_x: float32 [2048], P('bx'), may hold values from 0.05 to 4
- eigen_y: float32 [2048], P('by'), may hold values from 0.05 to 4
- eigen_z: float32 [4], replicated, may hold values from 0.05 to 4
Outputs:
- corrected: float32 [4, 2048, 2048], P(None, 'by', 'bx')
The draws below stay inside these ranges and needn't reach their ends.
All inputs are finite; a program needn't handle non-finite values.
Results may differ from the reference program's by a relative error of at most 0.0039.
Values may be sent and summed in bfloat16 or wider, within the bound.
A program may use at most 64 MiB of HBM per device.

```python
import math
import jax
import jax.numpy as jnp
from jax import lax

NX = 2048
NY = 2048
Z = 4
CLASSES = 8


def touch_ends(entries, key, low, high):
    longest = entries.shape.index(max(entries.shape))
    spots = []
    for shift in (0, 1):
        where = [jax.random.randint(jax.random.fold_in(key, axis), (), 0, length) for axis, length in enumerate(entries.shape)]
        where[longest] = (where[longest] + shift) % entries.shape[longest]
        spots.append(tuple(where))
    return entries.at[spots[0]].set(low).at[spots[1]].set(high)


def level_of(rng, extent, cuts, low, largest):
    def one(dim, blocks):
        heights = jax.random.uniform(jax.random.fold_in(jax.random.fold_in(rng, 6), dim), (blocks,), jnp.float32, low / len(cuts), largest / len(cuts))
        return jnp.repeat(jnp.exp(heights), extent[dim] // blocks).reshape((-1,) + (1,) * (len(extent) - dim - 1))

    factor_of = one(*cuts[0])
    for cut in cuts[1:]:
        factor_of = factor_of * one(*cut)
    return factor_of


def normal_values(rng, extent, width, limit, pieces=(), held_as=jnp.bfloat16):
    values = width * jax.random.normal(rng, extent, jnp.float32)
    if pieces:
        values = values * level_of(rng, extent, pieces, -0.22, 0.18)
    return jnp.clip(values, -limit, limit).astype(held_as)


def setup_inputs(seed: int = 0) -> dict:
    key_of = jax.random.split(jax.random.key(seed), 17)
    solution = normal_values(key_of[0], (Z, NY, NX), 1.0, 6.0, ((1, 32), (2, 16)), jnp.float32)
    source = normal_values(key_of[1], (Z, NY, NX), 2.0, 12.0, ((1, 32), (2, 16)), jnp.float32)
    class_ids = touch_ends(jax.random.randint(key_of[2], (Z, NY, NX), 0, CLASSES), jax.random.fold_in(key_of[2], 1), 0, CLASSES - 1).astype(jnp.int32)
    conductivity = jnp.clip(jnp.exp(jax.random.uniform(key_of[3], (CLASSES,), jnp.float32, math.log(0.3), math.log(3.0))), 0.3, 3.0)
    spacing_x = jnp.clip(jnp.exp(math.log(1.4) - 0.6931472 * jax.random.uniform(key_of[4], (NX,), jnp.float32) ** level_of(key_of[4], (NX,), ((0, 16),), -0.2, 0.2)), 0.7, 1.4)
    spacing_y = jnp.clip(jnp.exp(math.log(1.4) - 0.6931472 * jax.random.uniform(key_of[5], (NY,), jnp.float32) ** level_of(key_of[5], (NY,), ((0, 32),), -0.2, 0.2)), 0.7, 1.4)
    spacing_z = jnp.clip(jnp.exp(jax.random.uniform(key_of[6], (Z,), jnp.float32, math.log(0.7), math.log(1.4))), 0.7, 1.4)
    forward_x = normal_values(key_of[7], (NX, NX), NX ** -0.5, 0.125, ((0, 16),))
    forward_y = normal_values(key_of[8], (NY, NY), NY ** -0.5, 0.125, ((0, 32),))
    forward_z = normal_values(key_of[9], (Z, Z), Z ** -0.5, 3.0)
    inverse_x = normal_values(key_of[10], (NX, NX), NX ** -0.5, 0.125, ((0, 16),))
    inverse_y = normal_values(key_of[11], (NY, NY), NY ** -0.5, 0.125, ((0, 32),))
    inverse_z = normal_values(key_of[12], (Z, Z), Z ** -0.5, 3.0)
    eigen_x = jnp.clip(jnp.exp(math.log(4.0) - 4.3820266 * jax.random.uniform(key_of[13], (NX,), jnp.float32) ** level_of(key_of[13], (NX,), ((0, 16),), -0.2, 0.2)), 0.05, 4.0)
    eigen_y = jnp.clip(jnp.exp(math.log(4.0) - 4.3820266 * jax.random.uniform(key_of[14], (NY,), jnp.float32) ** level_of(key_of[14], (NY,), ((0, 32),), -0.2, 0.2)), 0.05, 4.0)
    eigen_z = jnp.clip(jnp.exp(jax.random.uniform(key_of[15], (Z,), jnp.float32, math.log(0.05), math.log(4.0))), 0.05, 4.0)
    return dict(solution=solution, source=source, class_ids=class_ids, conductivity=conductivity, spacing_x=spacing_x, spacing_y=spacing_y, spacing_z=spacing_z, forward_x=forward_x, forward_y=forward_y, forward_z=forward_z, inverse_x=inverse_x, inverse_y=inverse_y, inverse_z=inverse_z, eigen_x=eigen_x, eigen_y=eigen_y, eigen_z=eigen_z)


shift_value = 0.1


def coefficients(class_ids, conductivity):
    result = jnp.zeros(class_ids.shape, jnp.float32)
    for index in range(CLASSES):
        result = result + jnp.where(class_ids == index, conductivity[index], jnp.float32(0.0))
    return result


def operate(field, coef):
    padded = jnp.pad(field, 1)
    padcoef = jnp.pad(coef, 1)
    center = padded[1:-1, 1:-1, 1:-1]
    ccoef = padcoef[1:-1, 1:-1, 1:-1]
    slices = [(slice(2, None), slice(1, -1), slice(1, -1)), (slice(0, -2), slice(1, -1), slice(1, -1)),
              (slice(1, -1), slice(2, None), slice(1, -1)), (slice(1, -1), slice(0, -2), slice(1, -1)),
              (slice(1, -1), slice(1, -1), slice(2, None)), (slice(1, -1), slice(1, -1), slice(0, -2))]
    result = jnp.zeros(field.shape, jnp.float32)
    for where_at in slices:
        neighbour = padded[where_at]
        ncoef = padcoef[where_at]
        face = jnp.where(ncoef > 0, 2.0 * ccoef * ncoef / (ccoef + ncoef), ccoef)
        result = result + face * (center - neighbour)
    return result


def reference(solution, source, class_ids, conductivity, spacing_x, spacing_y, spacing_z, forward_x, forward_y, forward_z, inverse_x, inverse_y, inverse_z, eigen_x, eigen_y, eigen_z):
    highest = lax.Precision.HIGHEST
    coef = coefficients(class_ids, conductivity)
    operated = operate(solution, coef)
    weights = spacing_z[:, None, None] * spacing_y[None, :, None] * spacing_x[None, None, :]
    restricted = (weights * (source - operated)).astype(jnp.bfloat16)
    half = jnp.einsum('kji,mi->kjm', restricted.astype(jnp.float32), forward_x.astype(jnp.float32), precision=highest)
    modes_xy = jnp.einsum('kjm,nj->knm', half, forward_y.astype(jnp.float32), precision=highest)
    modes = jnp.einsum('qk,knm->qnm', forward_z.astype(jnp.float32), modes_xy, precision=highest)
    divisor = eigen_x[None, None, :] + eigen_y[None, :, None] + eigen_z[:, None, None] + shift_value
    scaled = modes / divisor
    spectral = jnp.einsum('kq,qnm->knm', inverse_z.astype(jnp.float32), scaled, precision=highest).astype(jnp.bfloat16)
    partial_x = jnp.einsum('knm,im->kni', spectral.astype(jnp.float32), inverse_x.astype(jnp.float32), precision=highest)
    field = jnp.einsum('kni,jn->kji', partial_x, inverse_y.astype(jnp.float32), precision=highest)
    return solution + weights * field
```

```python
import functools

import jax
import jax.numpy as jnp
from jax import lax
from jax.experimental import pallas as pl
from jax.experimental.pallas import tpu as pltpu
from jax.sharding import PartitionSpec as P

CLASSES = 8
SHIFT = 0.1
SUBS = 4
MESH = pl.DeviceIdType.MESH
F32 = jnp.float32
BF16 = jnp.bfloat16


def dot(a, b):
    return lax.dot_general(a, b, (((1,), (0,)), ((), ())), preferred_element_type=F32)


def dot_t(a, b):
    return lax.dot_general(a, b, (((1,), (1,)), ((), ())), preferred_element_type=F32)


def iota(shape, dim):
    return lax.broadcasted_iota(jnp.int32, shape, dim)


def to_row(column, width):
    size = column.shape[0]
    spread = jnp.where(iota((size, width), 0) == iota((size, width), 1), column, 0.0)
    return jnp.sum(spread, axis=0, keepdims=True)


def to_column(row, size):
    width = row.shape[1]
    spread = jnp.where(iota((size, width), 0) == iota((size, width), 1), row, 0.0)
    return jnp.sum(spread, axis=1, keepdims=True)


def face(c, cn):
    return jnp.where(cn > 0, 2.0 * c * cn / (c + cn), c)


def remote(src, dst, send, recv, **where):
    return pltpu.make_async_remote_copy(
        src_ref=src, dst_ref=dst, send_sem=send, recv_sem=recv, device_id=where, device_id_type=MESH
    )


def kernel(
    nbx,
    nby,
    sol_ref,
    src_ref,
    cls_ref,
    cond_ref,
    sx_ref,
    sy_ref,
    sz_ref,
    fx_ref,
    fy_ref,
    fz_ref,
    ix_ref,
    iy_ref,
    iz_ref,
    ex_ref,
    ey_ref,
    ez_ref,
    out_ref,
    coef,
    acc,
    xmsg,
    ymsg,
    xhalo,
    yhalo,
    raw_y,
    keep_y,
    pass_y,
    all_x,
    all_ex,
    pencil,
    half_out,
    half_in,
    tsend,
    tall,
    sall,
    uside,
    halo_send,
    halo_recv,
    load_sem,
    wy_send,
    wy_recv,
    wx_send,
    wx_recv,
    ring_send,
    ring_recv,
    half_send,
    half_recv,
    t_send,
    t_recv,
    s_send,
    s_recv,
    u_send,
    u_recv,
):
    bx, by = lax.axis_index("bx"), lax.axis_index("by")
    nz, nchip = nby // 2, nbx // 2
    z, xh = by // 2, by % 2
    chip, core = bx // 2, bx % 2
    other, sibling = by + 1 - 2 * xh, bx + 1 - 2 * core
    planes, rows, lanes = sol_ref.shape
    sub = rows // SUBS
    quarter = rows // 2

    barrier = pltpu.get_barrier_semaphore()

    def greet(o, _):
        pl.semaphore_signal(
            barrier, inc=1, device_id={"bx": (bx + o) % nbx}, device_id_type=MESH
        )
        return 0

    lax.fori_loop(1, nbx, greet, 0)
    near = (1, nby - 1, 2, nby - 2)
    for step in near:
        pl.semaphore_signal(
            barrier, inc=1, device_id={"by": (by + step) % nby}, device_id_type=MESH
        )

    loads = [
        pltpu.make_async_copy(fy_ref, raw_y.at[0], load_sem.at[0]),
        pltpu.make_async_copy(iy_ref, raw_y.at[1], load_sem.at[1]),
        pltpu.make_async_copy(fx_ref, all_x.at[0, core], load_sem.at[2]),
        pltpu.make_async_copy(ix_ref, all_x.at[1, core], load_sem.at[3]),
    ]
    for load in loads:
        load.start()

    for k in range(planes):
        ids = cls_ref[k]
        value = jnp.zeros(ids.shape, F32)
        for index in range(CLASSES):
            value = jnp.where(ids == index, cond_ref[index], value)
        coef[k] = value
    for which, ref in enumerate((sol_ref, coef)):
        for k in range(planes):
            row = which * planes + k
            v = ref[k]
            xmsg[0, pl.ds(row, 1), :] = to_row(v[:, 0:1], lanes)
            xmsg[1, pl.ds(row, 1), :] = to_row(v[:, lanes - 1 : lanes], lanes)
            ymsg[0, pl.ds(row, 1), :] = v[0:1, :]
            ymsg[1, pl.ds(row, 1), :] = v[rows - 1 : rows, :]

    all_ex[pl.ds(core, 1)] = ex_ref[...].reshape(1, 1, lanes)
    pl.semaphore_wait(barrier, nbx - 1 + len(near))

    halos = [
        remote(xmsg.at[0], xhalo.at[1], halo_send.at[0], halo_recv.at[0], bx=(bx + nbx - 1) % nbx),
        remote(xmsg.at[1], xhalo.at[0], halo_send.at[1], halo_recv.at[1], bx=(bx + 1) % nbx),
        remote(ymsg.at[0], yhalo.at[1], halo_send.at[2], halo_recv.at[2], by=(by + nby - 1) % nby),
        remote(ymsg.at[1], yhalo.at[0], halo_send.at[3], halo_recv.at[3], by=(by + 1) % nby),
    ]
    for copy in halos:
        copy.start()

    shares_x = [
        remote(fx_ref, all_x.at[0, core], wx_send.at[0], wx_recv.at[0], bx=sibling),
        remote(ix_ref, all_x.at[1, core], wx_send.at[1], wx_recv.at[1], bx=sibling),
        remote(all_ex.at[core], all_ex.at[core], wx_send.at[2], wx_recv.at[2], bx=sibling),
    ]
    for copy in shares_x:
        copy.start()

    shares_y = []
    low_lane = iota((rows, 128), 1) < 64
    for which in range(2):
        loads[which].wait()
        for pair in range(raw_y.shape[2] // 256):
            a = raw_y[which, :, 256 * pair : 256 * pair + 128].astype(F32)
            b = raw_y[which, :, 256 * pair + 128 : 256 * pair + 256].astype(F32)
            zero = jnp.where(low_lane, a, pltpu.roll(b, 64, 1))
            one = jnp.where(low_lane, pltpu.roll(a, 64, 1), b)
            where = slice(128 * pair, 128 * pair + 128)
            keep_y[which, pl.ds(xh, 1), :, where] = jnp.where(xh == 0, zero, one).astype(BF16)[None]
            pass_y[which, :, where] = jnp.where(xh == 0, one, zero).astype(BF16)
        copy = remote(
            pass_y.at[which], keep_y.at[which, xh], wy_send.at[which], wy_recv.at[which], by=other
        )
        copy.start()
        shares_y.append(copy)

    row_at, lane_at = iota((rows, lanes), 0), iota((rows, lanes), 1)
    for k in range(planes):
        u, c = sol_ref[k], coef[k]
        total = jnp.zeros((rows, lanes), F32)
        for n in (k + 1, k - 1):
            if 0 <= n < planes:
                total = total + face(c, coef[n]) * (u - sol_ref[n])
            else:
                total = total + c * u
        for dim, at, size in ((0, row_at, rows), (1, lane_at, lanes)):
            for shift, edge in ((1, 0), (size - 1, size - 1)):
                term = face(c, pltpu.roll(c, shift, dim)) * (u - pltpu.roll(u, shift, dim))
                total = total + jnp.where(at == edge, 0.0, term)
        acc[k] = total

    for copy in halos:
        copy.wait_recv()
    sides = (bx == 0, bx == nbx - 1, by == 0, by == nby - 1)
    ycol = to_column(sy_ref[...].reshape(1, rows), rows)
    area = ycol * sx_ref[...].reshape(1, lanes)
    for k in range(planes):
        u, c = sol_ref[k], coef[k]
        un, cn = [], []
        for side in range(2):
            halo = xhalo[side]
            gone = sides[side]
            un.append(jnp.where(gone, 0.0, to_column(halo[k : k + 1, :], rows)))
            cn.append(jnp.where(gone, 0.0, to_column(halo[planes + k : planes + k + 1, :], rows)))
        left = lane_at == 0
        term = face(c, jnp.where(left, cn[0], cn[1])) * (u - jnp.where(left, un[0], un[1]))
        total = acc[k] + jnp.where(left | (lane_at == lanes - 1), term, 0.0)
        for side, edge in ((0, 0), (1, rows - 1)):
            halo = yhalo[side]
            gone = sides[2 + side]
            un1 = jnp.where(gone, 0.0, halo[k : k + 1, :])
            cn1 = jnp.where(gone, 0.0, halo[planes + k : planes + k + 1, :])
            term = face(c, cn1) * (u - un1)
            total = total + jnp.where(row_at == edge, term, 0.0)
        value = (sz_ref[k] * area) * (src_ref[k] - total)
        at = pl.ds(pl.multiple_of(z * rows, rows), rows)
        pencil[0, at, k * lanes : (k + 1) * lanes] = value.astype(BF16)

    half = nz // 2

    def ring(phase):
        def hop(direction, d, s):
            sign = 1 - 2 * direction
            plane = (z - sign * d + 2 * nz) % nz
            part = (s + 2 * core) % SUBS
            at = pl.ds(pl.multiple_of(plane * rows + part * sub, sub), sub)
            view = pencil.at[phase, at, :]
            return remote(
                view,
                view,
                ring_send.at[phase, direction, d, s],
                ring_recv.at[phase, direction, d, s],
                by=(by + 2 * sign + nby) % nby,
            )

        def last(direction, s):
            return (s < SUBS // 2) == (direction == 0)

        for s in range(SUBS):
            for direction in range(2):
                hop(direction, 0, s).start()

        def step(d, _):
            for s in range(SUBS):
                for direction in range(2):
                    hop(direction, d - 1, s).wait_recv()
                    hop(direction, d, s).start()
            return 0

        lax.fori_loop(1, half - 1, step, 0)
        for s in range(SUBS):
            for direction in range(2):
                hop(direction, half - 2, s).wait_recv()
                if last(direction, s):
                    hop(direction, half - 1, s).start()
        for s in range(SUBS):
            for direction in range(2):
                if last(direction, s):
                    hop(direction, half - 1, s).wait_recv()

        def finish(d, _):
            for s in range(SUBS):
                for direction in range(2):
                    hop(direction, d, s).wait_send()
            return 0

        lax.fori_loop(0, half - 1, finish, 0)
        for s in range(SUBS):
            for direction in range(2):
                if last(direction, s):
                    hop(direction, half - 1, s).wait_send()

    def contract_y(phase):
        shares_y[phase].wait_recv()
        width = pencil.shape[2] // 2
        mine, copies = [], []
        for piece in range(2):
            at = slice(piece * width, (piece + 1) * width)
            whole = pencil[phase, :, at]
            gone = dot(keep_y[phase, 1 - xh], whole)
            half_out[phase, piece] = gone.astype(BF16)
            copy = remote(
                half_out.at[phase, piece],
                half_in.at[phase, piece],
                half_send.at[phase, piece],
                half_recv.at[phase, piece],
                by=other,
            )
            copy.start()
            copies.append(copy)
            mine.append(dot(keep_y[phase, xh], whole))
        for piece in range(2):
            copies[piece].wait_recv()
            mine[piece] = mine[piece] + half_in[phase, piece].astype(F32)
        for copy in copies:
            copy.wait_send()
        return [
            mine[k // (planes // 2)][:, (k % (planes // 2)) * lanes : (k % (planes // 2) + 1) * lanes]
            for k in range(planes)
        ]

    ring(0)
    modes_y = contract_y(0)

    for k in range(planes):
        for side in range(2):
            tsend[side, k * quarter : (k + 1) * quarter, :] = modes_y[k][
                side * quarter : (side + 1) * quarter, :
            ].astype(BF16)

    def t_copy(o):
        to = (bx + o) % nbx
        return remote(tsend.at[to % 2], tall.at[bx], t_send.at[o], t_recv.at[o], bx=to)

    def start_t(o, _):
        t_copy(o).start()
        return 0

    lax.fori_loop(1, nbx, start_t, 0)
    tall[pl.ds(bx, 1)] = tsend[pl.ds(core, 1)]
    for load in loads[2:]:
        load.wait()
    for copy in shares_x:
        copy.wait_recv()

    def wait_t(o, _):
        t_copy(o).wait_recv()
        return 0

    lax.fori_loop(1, nbx, wait_t, 0)
    rows_x = jnp.concatenate([tall[n] for n in range(nbx)], axis=1)
    half_modes = dot_t(rows_x, all_x[0].reshape(2 * lanes, all_x.shape[3]))

    planes_xy = [half_modes[k * quarter : (k + 1) * quarter, :] for k in range(planes)]
    ey = to_column(ey_ref[...].reshape(1, rows), rows)
    ey = jnp.where(core == 0, ey[:quarter], ey[quarter:])
    ex = jnp.concatenate([all_ex[0], all_ex[1]], axis=1)
    fz, iz = fz_ref[...].astype(F32), iz_ref[...].astype(F32)
    scaled = []
    for q in range(planes):
        mode = sum(fz[q : q + 1, k : k + 1] * planes_xy[k] for k in range(planes))
        scaled.append(mode / (ex + ey + ez_ref[q] + SHIFT))
    for k in range(planes):
        value = sum(iz[k : k + 1, q : q + 1] * scaled[q] for q in range(planes))
        sall[pl.ds(chip, 1), k * quarter : (k + 1) * quarter, :] = value.astype(BF16)[None]

    def s_copy(o):
        to = (chip + o) % nchip
        return remote(
            sall.at[chip], sall.at[chip], s_send.at[o], s_recv.at[o], bx=to * 2 + core
        )

    def start_s(o, _):
        s_copy(o).start()
        return 0

    def wait_s(o, _):
        s_copy(o).wait_recv()
        return 0

    lax.fori_loop(1, nchip, start_s, 0)
    lax.fori_loop(1, nchip, wait_s, 0)
    rows_m = jnp.concatenate([sall[n] for n in range(nchip)], axis=1)
    cells_x = dot_t(rows_m, all_x[1].reshape(2 * lanes, all_x.shape[3])).astype(BF16)

    at = pl.ds(pl.multiple_of(z * rows + core * quarter, quarter), quarter)
    for k in range(planes):
        piece = cells_x[k * quarter : (k + 1) * quarter, :]
        low, high = piece[:, :lanes], piece[:, lanes:]
        pencil[1, at, k * lanes : (k + 1) * lanes] = jnp.where(core == 0, low, high)
        uside[:, k * lanes : (k + 1) * lanes] = jnp.where(core == 0, high, low)
    copy = remote(uside, pencil.at[1, at, :], u_send.at[0], u_recv.at[0], bx=sibling)
    copy.start()
    copy.wait()

    ring(1)
    field = contract_y(1)
    for k in range(planes):
        out_ref[k] = sol_ref[k] + (sz_ref[k] * area) * field[k]

    for copy in halos + shares_x + shares_y:
        copy.wait_send()

    def end_t(o, _):
        t_copy(o).wait_send()
        return 0

    def end_s(o, _):
        s_copy(o).wait_send()
        return 0

    lax.fori_loop(1, nbx, end_t, 0)
    lax.fori_loop(1, nchip, end_s, 0)


def on_device(nbx, nby, *args):
    sol, forward_x, forward_y = args[0], args[7], args[8]
    planes, rows, lanes = sol.shape
    nx, ny = forward_x.shape[1], forward_y.shape[1]
    half = nby // 4
    quarter = rows // 2
    wide = planes * lanes
    vmem = pl.BlockSpec(memory_space=pltpu.VMEM)
    smem = pl.BlockSpec(memory_space=pltpu.SMEM)
    away = pl.BlockSpec(memory_space=pl.ANY)
    dma = pltpu.SemaphoreType.DMA
    specs = [vmem, vmem, vmem, smem, vmem, vmem, smem, away, away, vmem, away, away, vmem, vmem, vmem, smem]
    return pl.pallas_call(
        functools.partial(kernel, nbx, nby),
        out_shape=jax.ShapeDtypeStruct(sol.shape, F32),
        in_specs=specs,
        out_specs=vmem,
        scratch_shapes=[
            pltpu.VMEM((planes, rows, lanes), F32),
            pltpu.VMEM((planes, rows, lanes), F32),
            pltpu.VMEM((2, 2 * planes, lanes), F32),
            pltpu.VMEM((2, 2 * planes, lanes), F32),
            pltpu.VMEM((2, 2 * planes, lanes), F32),
            pltpu.VMEM((2, 2 * planes, lanes), F32),
            pltpu.VMEM((2, rows, ny), BF16),
            pltpu.VMEM((2, 2, rows, ny // 2), BF16),
            pltpu.VMEM((2, rows, ny // 2), BF16),
            pltpu.VMEM((2, 2, lanes, nx), BF16),
            pltpu.VMEM((2, 1, lanes), F32),
            pltpu.VMEM((2, ny // 2, wide), BF16),
            pltpu.VMEM((2, 2, rows, wide // 2), BF16),
            pltpu.VMEM((2, 2, rows, wide // 2), BF16),
            pltpu.VMEM((2, planes * quarter, lanes), BF16),
            pltpu.VMEM((nbx, planes * quarter, lanes), BF16),
            pltpu.VMEM((nbx // 2, planes * quarter, 2 * lanes), BF16),
            pltpu.VMEM((quarter, wide), BF16),
            dma((4,)),
            dma((4,)),
            dma((4,)),
            dma((2,)),
            dma((2,)),
            dma((3,)),
            dma((3,)),
            dma((2, 2, half, SUBS)),
            dma((2, 2, half, SUBS)),
            dma((2, 2)),
            dma((2, 2)),
            dma((nbx,)),
            dma((nbx,)),
            dma((nbx // 2,)),
            dma((nbx // 2,)),
            dma((1,)),
            dma((1,)),
        ],
        compiler_params=pltpu.CompilerParams(
            collective_id=0, has_side_effects=True, vmem_limit_bytes=40 << 20
        ),
    )(*args)


def solution(mesh):
    nbx, nby = mesh.shape["bx"], mesh.shape["by"]
    brick = P(None, "by", "bx")
    placed = (
        brick, brick, brick, P(), P("bx"), P("by"), P(), P("bx", None), P("by", None), P(),
        P("bx", None), P("by", None), P(), P("bx"), P("by"), P(),
    )
    return jax.shard_map(
        functools.partial(on_device, nbx, nby),
        mesh=mesh,
        in_specs=placed,
        out_specs=brick,
        check_vma=False,
    )
```

```python
import functools

import jax
import jax.numpy as jnp
from jax import lax
from jax.experimental import pallas as pl
from jax.experimental.pallas import tpu as pltpu
from jax.sharding import PartitionSpec as P

CLASSES = 8
SHIFT = 0.1
SUBS = 4
MESH = pl.DeviceIdType.MESH
F32 = jnp.float32
BF16 = jnp.bfloat16


def dot(a, b):
    return lax.dot_general(a, b, (((1,), (0,)), ((), ())), preferred_element_type=F32)


def dot_t(a, b):
    return lax.dot_general(a, b, (((1,), (1,)), ((), ())), preferred_element_type=F32)


def iota(shape, dim):
    return lax.broadcasted_iota(jnp.int32, shape, dim)


def to_row(column, width):
    size = column.shape[0]
    spread = jnp.where(iota((size, width), 0) == iota((size, width), 1), column, 0.0)
    return jnp.sum(spread, axis=0, keepdims=True)


def to_column(row, size):
    width = row.shape[1]
    spread = jnp.where(iota((size, width), 0) == iota((size, width), 1), row, 0.0)
    return jnp.sum(spread, axis=1, keepdims=True)


def face(c, cn):
    return jnp.where(cn > 0, 2.0 * c * cn / (c + cn), c)


def remote(src, dst, send, recv, **where):
    return pltpu.make_async_remote_copy(
        src_ref=src, dst_ref=dst, send_sem=send, recv_sem=recv, device_id=where, device_id_type=MESH
    )


def kernel(
    nbx,
    nby,
    sol_far,
    src_far,
    cls_far,
    cond_far,
    sx_far,
    sy_far,
    sz_far,
    fx_ref,
    fy_ref,
    fz_far,
    ix_ref,
    iy_ref,
    iz_far,
    ex_far,
    ey_far,
    ez_far,
    out_ref,
    sol_ref,
    src_ref,
    cls_ref,
    cond_ref,
    sx_ref,
    sy_ref,
    sz_ref,
    fz_ref,
    iz_ref,
    ex_ref,
    ey_ref,
    ez_ref,
    small_sem,
    coef,
    acc,
    xmsg,
    ymsg,
    xhalo,
    yhalo,
    raw_y,
    keep_y,
    pass_y,
    all_x,
    all_ex,
    pencil,
    half_out,
    half_in,
    tsend,
    tall,
    sall,
    uside,
    halo_send,
    halo_recv,
    load_sem,
    wy_send,
    wy_recv,
    wx_send,
    wx_recv,
    ring_send,
    ring_recv,
    half_send,
    half_recv,
    t_send,
    t_recv,
    s_send,
    s_recv,
    u_send,
    u_recv,
):
    bx, by = lax.axis_index("bx"), lax.axis_index("by")
    nz, nchip = nby // 2, nbx // 2
    z, xh = by // 2, by % 2
    chip, core = bx // 2, bx % 2
    other, sibling = by + 1 - 2 * xh, bx + 1 - 2 * core
    planes, rows, lanes = sol_ref.shape
    sub = rows // SUBS
    quarter = rows // 2

    barrier = pltpu.get_barrier_semaphore()

    def greet(o, _):
        pl.semaphore_signal(
            barrier, inc=1, device_id={"bx": (bx + o) % nbx}, device_id_type=MESH
        )
        return 0

    lax.fori_loop(1, nbx, greet, 0)
    near = (1, nby - 1, 2, nby - 2, 4, nby - 4, 6, nby - 6)
    for step in near:
        pl.semaphore_signal(
            barrier, inc=1, device_id={"by": (by + step) % nby}, device_id_type=MESH
        )

    smalls = [
        pltpu.make_async_copy(far, ref, small_sem.at[n])
        for n, (far, ref) in enumerate(
            (
                (cls_far, cls_ref),
                (cond_far, cond_ref),
                (sol_far, sol_ref),
                (ex_far, ex_ref),
                (src_far, src_ref),
                (sx_far, sx_ref),
                (sy_far, sy_ref),
                (sz_far, sz_ref),
                (fz_far, fz_ref),
                (iz_far, iz_ref),
                (ey_far, ey_ref),
                (ez_far, ez_ref),
            )
        )
    ]
    for load in smalls:
        load.start()
    loads = [
        pltpu.make_async_copy(fy_ref, raw_y.at[0], load_sem.at[0]),
        pltpu.make_async_copy(iy_ref, raw_y.at[1], load_sem.at[1]),
        pltpu.make_async_copy(fx_ref, all_x.at[0, core], load_sem.at[2]),
        pltpu.make_async_copy(ix_ref, all_x.at[1, core], load_sem.at[3]),
    ]
    for load in loads:
        load.start()

    for load in smalls[:4]:
        load.wait()
    for k in range(planes):
        ids = cls_ref[k]
        value = jnp.zeros(ids.shape, F32)
        for index in range(CLASSES):
            value = jnp.where(ids == index, cond_ref[index], value)
        coef[k] = value
    for which, ref in enumerate((sol_ref, coef)):
        for k in range(planes):
            row = which * planes + k
            v = ref[k]
            xmsg[0, pl.ds(row, 1), :] = to_row(v[:, 0:1], lanes)
            xmsg[1, pl.ds(row, 1), :] = to_row(v[:, lanes - 1 : lanes], lanes)
            ymsg[0, pl.ds(row, 1), :] = v[0:1, :]
            ymsg[1, pl.ds(row, 1), :] = v[rows - 1 : rows, :]

    all_ex[pl.ds(core, 1)] = ex_ref[...].reshape(1, 1, lanes)
    pl.semaphore_wait(barrier, nbx - 1 + len(near))

    halos = [
        remote(xmsg.at[0], xhalo.at[1], halo_send.at[0], halo_recv.at[0], bx=(bx + nbx - 1) % nbx),
        remote(xmsg.at[1], xhalo.at[0], halo_send.at[1], halo_recv.at[1], bx=(bx + 1) % nbx),
        remote(ymsg.at[0], yhalo.at[1], halo_send.at[2], halo_recv.at[2], by=(by + nby - 1) % nby),
        remote(ymsg.at[1], yhalo.at[0], halo_send.at[3], halo_recv.at[3], by=(by + 1) % nby),
    ]
    for copy in halos:
        copy.start()

    shares_x = [
        remote(fx_ref, all_x.at[0, core], wx_send.at[0], wx_recv.at[0], bx=sibling),
        remote(ix_ref, all_x.at[1, core], wx_send.at[1], wx_recv.at[1], bx=sibling),
        remote(all_ex.at[core], all_ex.at[core], wx_send.at[2], wx_recv.at[2], bx=sibling),
    ]
    for copy in shares_x:
        copy.start()

    shares_y = []
    low_lane = iota((rows, 128), 1) < 64
    for which in range(2):
        loads[which].wait()
        for pair in range(raw_y.shape[2] // 256):
            a = raw_y[which, :, 256 * pair : 256 * pair + 128].astype(F32)
            b = raw_y[which, :, 256 * pair + 128 : 256 * pair + 256].astype(F32)
            zero = jnp.where(low_lane, a, pltpu.roll(b, 64, 1))
            one = jnp.where(low_lane, pltpu.roll(a, 64, 1), b)
            where = slice(128 * pair, 128 * pair + 128)
            keep_y[which, pl.ds(xh, 1), :, where] = jnp.where(xh == 0, zero, one).astype(BF16)[None]
            pass_y[which, :, where] = jnp.where(xh == 0, one, zero).astype(BF16)
        copy = remote(
            pass_y.at[which], keep_y.at[which, xh], wy_send.at[which], wy_recv.at[which], by=other
        )
        copy.start()
        shares_y.append(copy)

    row_at, lane_at = iota((rows, lanes), 0), iota((rows, lanes), 1)
    for k in range(planes):
        u, c = sol_ref[k], coef[k]
        total = jnp.zeros((rows, lanes), F32)
        for n in (k + 1, k - 1):
            if 0 <= n < planes:
                total = total + face(c, coef[n]) * (u - sol_ref[n])
            else:
                total = total + c * u
        for dim, at, size in ((0, row_at, rows), (1, lane_at, lanes)):
            for shift, edge in ((1, 0), (size - 1, size - 1)):
                term = face(c, pltpu.roll(c, shift, dim)) * (u - pltpu.roll(u, shift, dim))
                total = total + jnp.where(at == edge, 0.0, term)
        acc[k] = total

    for load in smalls[4:]:
        load.wait()
    for copy in halos:
        copy.wait_recv()
    sides = (bx == 0, bx == nbx - 1, by == 0, by == nby - 1)
    ycol = to_column(sy_ref[...].reshape(1, rows), rows)
    area = ycol * sx_ref[...].reshape(1, lanes)
    for k in range(planes):
        u, c = sol_ref[k], coef[k]
        un, cn = [], []
        for side in range(2):
            halo = xhalo[side]
            gone = sides[side]
            un.append(jnp.where(gone, 0.0, to_column(halo[k : k + 1, :], rows)))
            cn.append(jnp.where(gone, 0.0, to_column(halo[planes + k : planes + k + 1, :], rows)))
        left = lane_at == 0
        term = face(c, jnp.where(left, cn[0], cn[1])) * (u - jnp.where(left, un[0], un[1]))
        total = acc[k] + jnp.where(left | (lane_at == lanes - 1), term, 0.0)
        for side, edge in ((0, 0), (1, rows - 1)):
            halo = yhalo[side]
            gone = sides[2 + side]
            un1 = jnp.where(gone, 0.0, halo[k : k + 1, :])
            cn1 = jnp.where(gone, 0.0, halo[planes + k : planes + k + 1, :])
            term = face(c, cn1) * (u - un1)
            total = total + jnp.where(row_at == edge, term, 0.0)
        value = (sz_ref[k] * area) * (src_ref[k] - total)
        at = pl.ds(pl.multiple_of(z * rows, rows), rows)
        pencil[0, at, k * lanes : (k + 1) * lanes] = value.astype(BF16)

    def ring(phase):
        def hop(number, behind, ahead, s):
            plane = (z - behind + 2 * nz) % nz
            part = (s + 2 * core) % SUBS
            at = pl.ds(pl.multiple_of(plane * rows + part * sub, sub), sub)
            view = pencil.at[phase, at, :]
            return remote(
                view,
                view,
                ring_send.at[phase, number, s],
                ring_recv.at[phase, (behind + ahead) % nz, s],
                by=(by + 2 * ahead + nby) % nby,
            )

        def arrive(behind, s):
            hop(0, behind, 0, s).wait_recv()

        parts = range(SUBS)
        for s in parts:
            for number, ahead in enumerate((3, -3)):
                hop(number, 0, ahead, s).start()
        for s in parts:
            for number, ahead in enumerate((1, -1)):
                hop(2 + number, 0, ahead, s).start()
        for s in parts:
            for side, sign in enumerate((1, -1)):
                arrive(3 * sign, s)
                for number, ahead in enumerate((3 * sign, sign, -sign)):
                    hop(4 + 3 * side + number, 3 * sign, ahead, s).start()
        for s in parts:
            for side, sign in enumerate((1, -1)):
                arrive(6 * sign, s)
                for number, ahead in enumerate((sign, -sign)):
                    hop(10 + 2 * side + number, 6 * sign, ahead, s).start()
                if (s < SUBS // 2) == (side == 0):
                    hop(14, 6 * sign, 2 * sign, s).start()
        for behind in (1, 2, 4, 5, 7):
            for s in parts:
                for sign in (1, -1):
                    arrive(behind * sign, s)
        for s in parts:
            arrive(8, s)

        def finish(number, _):
            for s in parts:
                hop(number, 0, 1, s).wait_send()
            return 0

        lax.fori_loop(0, 15, finish, 0)

    def contract_y(phase):
        shares_y[phase].wait_recv()
        width = pencil.shape[2] // 2
        mine, copies = [], []
        for piece in range(2):
            at = slice(piece * width, (piece + 1) * width)
            whole = pencil[phase, :, at]
            gone = dot(keep_y[phase, 1 - xh], whole)
            half_out[phase, piece] = gone.astype(BF16)
            copy = remote(
                half_out.at[phase, piece],
                half_in.at[phase, piece],
                half_send.at[phase, piece],
                half_recv.at[phase, piece],
                by=other,
            )
            copy.start()
            copies.append(copy)
            mine.append(dot(keep_y[phase, xh], whole))
        for piece in range(2):
            copies[piece].wait_recv()
            mine[piece] = mine[piece] + half_in[phase, piece].astype(F32)
        for copy in copies:
            copy.wait_send()
        return [
            mine[k // (planes // 2)][:, (k % (planes // 2)) * lanes : (k % (planes // 2) + 1) * lanes]
            for k in range(planes)
        ]

    ring(0)
    modes_y = contract_y(0)

    for k in range(planes):
        for side in range(2):
            tsend[side, k * quarter : (k + 1) * quarter, :] = modes_y[k][
                side * quarter : (side + 1) * quarter, :
            ].astype(BF16)

    def t_copy(o):
        to = (bx + o) % nbx
        return remote(tsend.at[to % 2], tall.at[bx], t_send.at[o], t_recv.at[o], bx=to)

    def start_t(o, _):
        t_copy(o).start()
        return 0

    lax.fori_loop(1, nbx, start_t, 0)
    tall[pl.ds(bx, 1)] = tsend[pl.ds(core, 1)]
    for load in loads[2:]:
        load.wait()
    for copy in shares_x:
        copy.wait_recv()

    def wait_t(o, _):
        t_copy(o).wait_recv()
        return 0

    lax.fori_loop(1, nbx, wait_t, 0)
    rows_x = jnp.concatenate([tall[n] for n in range(nbx)], axis=1)
    half_modes = dot_t(rows_x, all_x[0].reshape(2 * lanes, all_x.shape[3]))

    planes_xy = [half_modes[k * quarter : (k + 1) * quarter, :] for k in range(planes)]
    ey = to_column(ey_ref[...].reshape(1, rows), rows)
    ey = jnp.where(core == 0, ey[:quarter], ey[quarter:])
    ex = jnp.concatenate([all_ex[0], all_ex[1]], axis=1)
    fz, iz = fz_ref[...].astype(F32), iz_ref[...].astype(F32)
    scaled = []
    for q in range(planes):
        mode = sum(fz[q : q + 1, k : k + 1] * planes_xy[k] for k in range(planes))
        scaled.append(mode / (ex + ey + ez_ref[q] + SHIFT))
    for k in range(planes):
        value = sum(iz[k : k + 1, q : q + 1] * scaled[q] for q in range(planes))
        sall[pl.ds(chip, 1), k * quarter : (k + 1) * quarter, :] = value.astype(BF16)[None]

    def s_copy(o):
        to = (chip + o) % nchip
        return remote(
            sall.at[chip], sall.at[chip], s_send.at[o], s_recv.at[o], bx=to * 2 + core
        )

    def start_s(o, _):
        s_copy(o).start()
        return 0

    def wait_s(o, _):
        s_copy(o).wait_recv()
        return 0

    lax.fori_loop(1, nchip, start_s, 0)
    lax.fori_loop(1, nchip, wait_s, 0)
    rows_m = jnp.concatenate([sall[n] for n in range(nchip)], axis=1)
    cells_x = dot_t(rows_m, all_x[1].reshape(2 * lanes, all_x.shape[3])).astype(BF16)

    at = pl.ds(pl.multiple_of(z * rows + core * quarter, quarter), quarter)
    for k in range(planes):
        piece = cells_x[k * quarter : (k + 1) * quarter, :]
        low, high = piece[:, :lanes], piece[:, lanes:]
        pencil[1, at, k * lanes : (k + 1) * lanes] = jnp.where(core == 0, low, high)
        uside[:, k * lanes : (k + 1) * lanes] = jnp.where(core == 0, high, low)
    copy = remote(uside, pencil.at[1, at, :], u_send.at[0], u_recv.at[0], bx=sibling)
    copy.start()
    copy.wait()

    ring(1)
    field = contract_y(1)
    for k in range(planes):
        out_ref[k] = sol_ref[k] + (sz_ref[k] * area) * field[k]

    for copy in halos + shares_x + shares_y:
        copy.wait_send()

    def end_t(o, _):
        t_copy(o).wait_send()
        return 0

    def end_s(o, _):
        s_copy(o).wait_send()
        return 0

    lax.fori_loop(1, nbx, end_t, 0)
    lax.fori_loop(1, nchip, end_s, 0)


def on_device(nbx, nby, *args):
    sol, forward_x = args[0], args[7]
    planes, rows, lanes = sol.shape
    nx, ny = forward_x.shape[1], rows * nby
    quarter = rows // 2
    wide = planes * lanes
    vmem = pl.BlockSpec(memory_space=pltpu.VMEM)
    far = pl.BlockSpec(memory_space=pltpu.HBM)
    dma = pltpu.SemaphoreType.DMA
    near = [pltpu.VMEM] * 3 + [pltpu.SMEM] + [pltpu.VMEM] * 2 + [pltpu.SMEM]
    near += [None] * 2 + [pltpu.VMEM] + [None] * 2 + [pltpu.VMEM] * 3 + [pltpu.SMEM]
    return pl.pallas_call(
        functools.partial(kernel, nbx, nby),
        out_shape=jax.ShapeDtypeStruct(sol.shape, F32),
        in_specs=[far] * len(args),
        out_specs=vmem,
        scratch_shapes=[space(arg.shape, arg.dtype) for space, arg in zip(near, args) if space]
        + [
            dma((12,)),
            pltpu.VMEM((planes, rows, lanes), F32),
            pltpu.VMEM((planes, rows, lanes), F32),
            pltpu.VMEM((2, 2 * planes, lanes), F32),
            pltpu.VMEM((2, 2 * planes, lanes), F32),
            pltpu.VMEM((2, 2 * planes, lanes), F32),
            pltpu.VMEM((2, 2 * planes, lanes), F32),
            pltpu.VMEM((2, rows, ny), BF16),
            pltpu.VMEM((2, 2, rows, ny // 2), BF16),
            pltpu.VMEM((2, rows, ny // 2), BF16),
            pltpu.VMEM((2, 2, lanes, nx), BF16),
            pltpu.VMEM((2, 1, lanes), F32),
            pltpu.VMEM((2, ny // 2, wide), BF16),
            pltpu.VMEM((2, 2, rows, wide // 2), BF16),
            pltpu.VMEM((2, 2, rows, wide // 2), BF16),
            pltpu.VMEM((2, planes * quarter, lanes), BF16),
            pltpu.VMEM((nbx, planes * quarter, lanes), BF16),
            pltpu.VMEM((nbx // 2, planes * quarter, 2 * lanes), BF16),
            pltpu.VMEM((quarter, wide), BF16),
            dma((4,)),
            dma((4,)),
            dma((4,)),
            dma((2,)),
            dma((2,)),
            dma((3,)),
            dma((3,)),
            dma((2, nby // 2 - 1, SUBS)),
            dma((2, nby // 2, SUBS)),
            dma((2, 2)),
            dma((2, 2)),
            dma((nbx,)),
            dma((nbx,)),
            dma((nbx // 2,)),
            dma((nbx // 2,)),
            dma((1,)),
            dma((1,)),
        ],
        compiler_params=pltpu.CompilerParams(
            collective_id=0, has_side_effects=True, vmem_limit_bytes=60 << 20
        ),
    )(*args)


def solution(mesh):
    nbx, nby = mesh.shape["bx"], mesh.shape["by"]
    brick = P(None, "by", "bx")
    placed = (
        brick, brick, brick, P(), P("bx"), P("by"), P(), P("bx", None), P("by", None), P(),
        P("bx", None), P("by", None), P(), P("bx"), P("by"), P(),
    )
    return jax.shard_map(
        functools.partial(on_device, nbx, nby),
        mesh=mesh,
        in_specs=placed,
        out_specs=brick,
        check_vma=False,
    )
```

```python
import functools

import jax
import jax.numpy as jnp
from jax import lax
from jax.experimental import pallas as pl
from jax.experimental.pallas import tpu as pltpu
from jax.sharding import PartitionSpec as P

CLASSES = 8
SHIFT = 0.1
SUBS = 2
MESH = pl.DeviceIdType.MESH
F32 = jnp.float32
BF16 = jnp.bfloat16


def dot(a, b):
    return lax.dot_general(a, b, (((1,), (0,)), ((), ())), preferred_element_type=F32)


def dot_t(a, b):
    return lax.dot_general(a, b, (((1,), (1,)), ((), ())), preferred_element_type=F32)


def iota(shape, dim):
    return lax.broadcasted_iota(jnp.int32, shape, dim)


def to_row(column, width):
    size = column.shape[0]
    spread = jnp.where(iota((size, width), 0) == iota((size, width), 1), column, 0.0)
    return jnp.sum(spread, axis=0, keepdims=True)


def to_column(row, size):
    width = row.shape[1]
    spread = jnp.where(iota((size, width), 0) == iota((size, width), 1), row, 0.0)
    return jnp.sum(spread, axis=1, keepdims=True)


def face(c, cn):
    return jnp.where(cn > 0, 2.0 * c * cn / (c + cn), c)


def remote(src, dst, send, recv, **where):
    return pltpu.make_async_remote_copy(
        src_ref=src, dst_ref=dst, send_sem=send, recv_sem=recv, device_id=where, device_id_type=MESH
    )


def kernel(
    nbx,
    nby,
    sol_far,
    src_far,
    cls_far,
    cond_far,
    sx_far,
    sy_far,
    sz_far,
    fx_ref,
    fy_ref,
    fz_far,
    ix_ref,
    iy_ref,
    iz_far,
    ex_far,
    ey_far,
    ez_far,
    out_ref,
    sol_ref,
    src_ref,
    cls_ref,
    cond_ref,
    sx_ref,
    sy_ref,
    sz_ref,
    fz_ref,
    iz_ref,
    ex_ref,
    ey_ref,
    ez_ref,
    small_sem,
    coef,
    acc,
    xmsg,
    ymsg,
    xhalo,
    yhalo,
    raw_y,
    keep_y,
    pass_y,
    all_x,
    all_ex,
    pencil,
    half_out,
    half_in,
    tsend,
    tall,
    sall,
    uside,
    halo_send,
    halo_recv,
    load_sem,
    wy_send,
    wy_recv,
    wx_send,
    wx_recv,
    ring_send,
    ring_recv,
    half_send,
    half_recv,
    t_send,
    t_recv,
    s_send,
    s_recv,
    u_send,
    u_recv,
):
    bx, by = lax.axis_index("bx"), lax.axis_index("by")
    nz, ny4 = nby // 2, nbx // 4
    z, xh = by // 2, by % 2
    xl, row4, core = bx // (2 * ny4), (bx // 2) % ny4, bx % 2
    mine4 = 2 * xl + core
    other = by + 1 - 2 * xh

    def relative(j):
        xl2 = xl if j < 2 else 1 - xl
        core2 = core if j % 2 == 0 else 1 - core
        return (xl2 * ny4 + row4) * 2 + core2, 2 * xl2 + core2

    planes, rows, lanes = sol_ref.shape
    sub = rows // SUBS
    quarter = rows // 4

    barrier = pltpu.get_barrier_semaphore()

    def greet(o, _):
        pl.semaphore_signal(
            barrier, inc=1, device_id={"bx": (bx + o) % nbx}, device_id_type=MESH
        )
        pl.semaphore_signal(
            barrier, inc=1, device_id={"bx": (bx + o) % nbx, "by": other}, device_id_type=MESH
        )
        return 0

    lax.fori_loop(1, nbx, greet, 0)
    near = (1, nby - 1, 2, nby - 2, 4, nby - 4, 6, nby - 6)
    for step in near:
        pl.semaphore_signal(
            barrier, inc=1, device_id={"by": (by + step) % nby}, device_id_type=MESH
        )

    smalls = [
        pltpu.make_async_copy(far, ref, small_sem.at[n])
        for n, (far, ref) in enumerate(
            (
                (cls_far, cls_ref),
                (cond_far, cond_ref),
                (sol_far, sol_ref),
                (ex_far, ex_ref),
                (src_far, src_ref),
                (sx_far, sx_ref),
                (sy_far, sy_ref),
                (sz_far, sz_ref),
                (fz_far, fz_ref),
                (iz_far, iz_ref),
                (ey_far, ey_ref),
                (ez_far, ez_ref),
            )
        )
    ]
    for load in smalls:
        load.start()
    loads = [
        pltpu.make_async_copy(fy_ref, raw_y.at[0], load_sem.at[0]),
        pltpu.make_async_copy(iy_ref, raw_y.at[1], load_sem.at[1]),
        pltpu.make_async_copy(fx_ref, all_x.at[0, mine4], load_sem.at[2]),
        pltpu.make_async_copy(ix_ref, all_x.at[1, mine4], load_sem.at[3]),
    ]
    for load in loads:
        load.start()

    for load in smalls[:4]:
        load.wait()
    for k in range(planes):
        ids = cls_ref[k]
        value = jnp.zeros(ids.shape, F32)
        for index in range(CLASSES):
            value = jnp.where(ids == index, cond_ref[index], value)
        coef[k] = value
    for which, ref in enumerate((sol_ref, coef)):
        for k in range(planes):
            row = which * planes + k
            v = ref[k]
            xmsg[0, pl.ds(row, 1), :] = to_row(v[:, 0:1], lanes)
            xmsg[1, pl.ds(row, 1), :] = to_row(v[:, lanes - 1 : lanes], lanes)
            ymsg[0, pl.ds(row, 1), :] = v[0:1, :]
            ymsg[1, pl.ds(row, 1), :] = v[rows - 1 : rows, :]

    all_ex[pl.ds(mine4, 1)] = ex_ref[...].reshape(1, 1, lanes)
    pl.semaphore_wait(barrier, 2 * (nbx - 1) + len(near))

    halos = [
        remote(xmsg.at[0], xhalo.at[1], halo_send.at[0], halo_recv.at[0], bx=(bx + nbx - 1) % nbx),
        remote(xmsg.at[1], xhalo.at[0], halo_send.at[1], halo_recv.at[1], bx=(bx + 1) % nbx),
        remote(ymsg.at[0], yhalo.at[1], halo_send.at[2], halo_recv.at[2], by=(by + nby - 1) % nby),
        remote(ymsg.at[1], yhalo.at[0], halo_send.at[3], halo_recv.at[3], by=(by + 1) % nby),
    ]
    for copy in halos:
        copy.start()

    shares_y = []
    low_lane = iota((rows, 128), 1) < 64
    for which in range(2):
        loads[which].wait()
        for pair in range(raw_y.shape[2] // 256):
            a = raw_y[which, :, 256 * pair : 256 * pair + 128].astype(F32)
            b = raw_y[which, :, 256 * pair + 128 : 256 * pair + 256].astype(F32)
            zero = jnp.where(low_lane, a, pltpu.roll(b, 64, 1))
            one = jnp.where(low_lane, pltpu.roll(a, 64, 1), b)
            where = slice(128 * pair, 128 * pair + 128)
            keep_y[which, pl.ds(xh, 1), :, where] = jnp.where(xh == 0, zero, one).astype(BF16)[None]
            pass_y[which, :, where] = jnp.where(xh == 0, one, zero).astype(BF16)
        copy = remote(
            pass_y.at[which], keep_y.at[which, xh], wy_send.at[which], wy_recv.at[which], by=other
        )
        copy.start()
        shares_y.append(copy)

    row_at, lane_at = iota((rows, lanes), 0), iota((rows, lanes), 1)
    for k in range(planes):
        u, c = sol_ref[k], coef[k]
        total = jnp.zeros((rows, lanes), F32)
        for n in (k + 1, k - 1):
            if 0 <= n < planes:
                total = total + face(c, coef[n]) * (u - sol_ref[n])
            else:
                total = total + c * u
        for dim, at, size in ((0, row_at, rows), (1, lane_at, lanes)):
            for shift, edge in ((1, 0), (size - 1, size - 1)):
                term = face(c, pltpu.roll(c, shift, dim)) * (u - pltpu.roll(u, shift, dim))
                total = total + jnp.where(at == edge, 0.0, term)
        acc[k] = total

    for load in smalls[4:]:
        load.wait()
    for copy in halos:
        copy.wait_recv()

    shares_x = []
    for which, ref in enumerate((fx_ref, ix_ref)):
        for j in (1, 2):
            at, number = all_x.at[which, mine4], 3 * which + j - 1
            shares_x.append(
                remote(ref, at, wx_send.at[number], wx_recv.at[number], bx=relative(j)[0])
            )
    for j in (1, 2, 3):
        at, number = all_ex.at[mine4], 5 + j
        shares_x.append(remote(at, at, wx_send.at[number], wx_recv.at[number], bx=relative(j)[0]))
    for copy in shares_x[4:] + shares_x[:4]:
        copy.start()

    def pass_x(which):
        at, number = all_x.at[which, relative(2)[1]], 3 * which + 2
        return remote(at, at, wx_send.at[number], wx_recv.at[number], bx=relative(1)[0])

    sides = (bx == 0, bx == nbx - 1, by == 0, by == nby - 1)
    ycol = to_column(sy_ref[...].reshape(1, rows), rows)
    area = ycol * sx_ref[...].reshape(1, lanes)
    for k in range(planes):
        u, c = sol_ref[k], coef[k]
        un, cn = [], []
        for side in range(2):
            halo = xhalo[side]
            gone = sides[side]
            un.append(jnp.where(gone, 0.0, to_column(halo[k : k + 1, :], rows)))
            cn.append(jnp.where(gone, 0.0, to_column(halo[planes + k : planes + k + 1, :], rows)))
        left = lane_at == 0
        term = face(c, jnp.where(left, cn[0], cn[1])) * (u - jnp.where(left, un[0], un[1]))
        total = acc[k] + jnp.where(left | (lane_at == lanes - 1), term, 0.0)
        for side, edge in ((0, 0), (1, rows - 1)):
            halo = yhalo[side]
            gone = sides[2 + side]
            un1 = jnp.where(gone, 0.0, halo[k : k + 1, :])
            cn1 = jnp.where(gone, 0.0, halo[planes + k : planes + k + 1, :])
            term = face(c, cn1) * (u - un1)
            total = total + jnp.where(row_at == edge, term, 0.0)
        value = (sz_ref[k] * area) * (src_ref[k] - total)
        at = pl.ds(pl.multiple_of(z * rows, rows), rows)
        pencil[0, at, k * lanes : (k + 1) * lanes] = value.astype(BF16)

    def ring(phase, ready=None):
        def hop(number, behind, ahead, s):
            plane = (z - behind + 2 * nz) % nz
            part = (s + xl * (SUBS // 2)) % SUBS
            at = pl.ds(pl.multiple_of(plane * rows + part * sub, sub), sub)
            view = pencil.at[phase, at, :]
            return remote(
                view,
                view,
                ring_send.at[phase, number, s],
                ring_recv.at[phase, (behind + ahead) % nz, s],
                by=(by + 2 * ahead + nby) % nby,
            )

        def arrive(behind, s):
            hop(0, behind, 0, s).wait_recv()

        parts = range(SUBS)
        for s in parts:
            if ready is not None:
                ready(s)
            for number, ahead in enumerate((3, -3)):
                hop(number, 0, ahead, s).start()
        for s in parts:
            for number, ahead in enumerate((1, -1)):
                hop(2 + number, 0, ahead, s).start()
        for s in parts:
            for side, sign in enumerate((1, -1)):
                arrive(3 * sign, s)
                for number, ahead in enumerate((3 * sign, sign, -sign)):
                    hop(4 + 3 * side + number, 3 * sign, ahead, s).start()
        for s in parts:
            for side, sign in enumerate((1, -1)):
                arrive(6 * sign, s)
                for number, ahead in enumerate((sign, -sign)):
                    hop(10 + 2 * side + number, 6 * sign, ahead, s).start()
                if (s < SUBS // 2) == (side == 0):
                    hop(14, 6 * sign, 2 * sign, s).start()
        for behind in (1, 2, 4, 5, 7):
            for s in parts:
                for sign in (1, -1):
                    arrive(behind * sign, s)
        for s in parts:
            arrive(8, s)

        def finish(number, _):
            for s in parts:
                hop(number, 0, 1, s).wait_send()
            return 0

        lax.fori_loop(0, 15, finish, 0)

    def contract_y(phase):
        shares_y[phase].wait_recv()
        width = pencil.shape[2] // 2
        mine, copies = [], []
        for piece in range(2):
            at = slice(piece * width, (piece + 1) * width)
            whole = pencil[phase, :, at]
            gone = dot(keep_y[phase, 1 - xh], whole)
            half_out[phase, piece] = gone.astype(BF16)
            copy = remote(
                half_out.at[phase, piece],
                half_in.at[phase, piece],
                half_send.at[phase, piece],
                half_recv.at[phase, piece],
                by=other,
            )
            copy.start()
            copies.append(copy)
            mine.append(dot(keep_y[phase, xh], whole))
        for piece in range(2):
            copies[piece].wait_recv()
            mine[piece] = mine[piece] + half_in[phase, piece].astype(F32)
        for copy in copies:
            copy.wait_send()
        return [
            mine[k // (planes // 2)][:, (k % (planes // 2)) * lanes : (k % (planes // 2) + 1) * lanes]
            for k in range(planes)
        ]

    ring(0)
    shares_x[1].wait_recv()
    passed = [pass_x(0), pass_x(1)]
    passed[0].start()
    shares_y[0].wait_recv()
    sums = dot(keep_y[0].reshape(2 * rows, keep_y.shape[3]), pencil[0])

    for side in range(2):
        for r in range(4):
            for k in range(planes):
                tsend[side, r, k * quarter : (k + 1) * quarter, :] = sums[
                    side * rows + r * quarter : side * rows + (r + 1) * quarter,
                    k * lanes : (k + 1) * lanes,
                ].astype(BF16)

    def t_copy(t):
        to, cross = (bx + t) % nbx, t // nbx
        side = xh + cross - 2 * xh * cross
        r = 2 * (to // (2 * ny4)) + to % 2
        return pltpu.make_async_remote_copy(
            src_ref=tsend.at[side, r],
            dst_ref=tall.at[xh, bx],
            send_sem=t_send.at[t],
            recv_sem=t_recv.at[t],
            device_id={"bx": to, "by": 2 * z + side},
            device_id_type=MESH,
        )

    def start_t(t, _):
        t_copy(t).start()
        return 0

    def wait_t(t, _):
        t_copy(t).wait_recv()
        return 0

    lax.fori_loop(1, 2 * nbx, start_t, 0)
    tall[pl.ds(xh, 1), pl.ds(bx, 1)] = tsend[pl.ds(xh, 1), pl.ds(mine4, 1)]
    for load in loads[2:]:
        load.wait()
    shares_x[3].wait_recv()
    passed[1].start()
    for copy in (shares_x[0], shares_x[4], shares_x[5], shares_x[6], passed[0]):
        copy.wait_recv()
    lax.fori_loop(1, 2 * nbx, wait_t, 0)
    rows_x = jnp.concatenate(
        [jnp.concatenate([tall[side, n] for n in range(nbx)], axis=1) for side in range(2)], axis=0
    )
    both = dot_t(rows_x, all_x[0].reshape(4 * lanes, all_x.shape[3]))
    part_modes = both[: planes * quarter] + both[planes * quarter :]

    planes_xy = [part_modes[k * quarter : (k + 1) * quarter, :] for k in range(planes)]
    ey_all = to_column(ey_ref[...].reshape(1, rows), rows)
    ey = ey_all[:quarter]
    for r in range(1, 4):
        ey = jnp.where(mine4 == r, ey_all[r * quarter : (r + 1) * quarter], ey)
    ex = jnp.concatenate([all_ex[r] for r in range(4)], axis=1)
    fz, iz = fz_ref[...].astype(F32), iz_ref[...].astype(F32)
    scaled = []
    for q in range(planes):
        mode = sum(fz[q : q + 1, k : k + 1] * planes_xy[k] for k in range(planes))
        scaled.append(mode / (ex + ey + ez_ref[q] + SHIFT))
    for k in range(planes):
        value = sum(iz[k : k + 1, q : q + 1] * scaled[q] for q in range(planes))
        sall[pl.ds(row4, 1), k * quarter : (k + 1) * quarter, :] = value.astype(BF16)[None]

    s_copies = []
    for o in range(1, ny4):
        to = (row4 + o) % ny4
        at = sall.at[row4]
        s_copies.append(
            remote(at, at, s_send.at[o], s_recv.at[o], bx=(xl * ny4 + to) * 2 + core)
        )
    for copy in s_copies:
        copy.start()
    for copy in (shares_x[2], passed[1]):
        copy.wait_recv()
    for copy in s_copies:
        copy.wait_recv()
    rows_m = jnp.concatenate(
        [
            sall[n, :, (2 * side + c) * lanes : (2 * side + c + 1) * lanes]
            for side in range(2)
            for n in range(ny4)
            for c in range(2)
        ],
        axis=1,
    )
    cells_x = dot_t(rows_m, all_x[1].reshape(4 * lanes, all_x.shape[3])).astype(BF16)

    at = pl.ds(pl.multiple_of(z * rows + mine4 * quarter, quarter), quarter)
    for r in range(4):
        for k in range(planes):
            uside[r, :, k * lanes : (k + 1) * lanes] = cells_x[
                k * quarter : (k + 1) * quarter, r * lanes : (r + 1) * lanes
            ]
    u_copies = []
    for j in (2, 3, 1):
        to, r = relative(j)
        u_copies.append(
            remote(uside.at[r], pencil.at[1, at, :], u_send.at[j], u_recv.at[j], bx=to)
        )
    for copy in u_copies:
        copy.start()
    pencil[1, at, :] = uside[pl.ds(mine4, 1)].reshape(quarter, planes * lanes)

    def ready(s):
        for copy in u_copies[2:] if s == 0 else u_copies[:2]:
            copy.wait_recv()

    ring(1, ready)
    field = contract_y(1)
    for k in range(planes):
        out_ref[k] = sol_ref[k] + (sz_ref[k] * area) * field[k]

    for copy in halos + shares_x + shares_y + passed + s_copies + u_copies:
        copy.wait_send()

    def end_t(t, _):
        t_copy(t).wait_send()
        return 0

    lax.fori_loop(1, 2 * nbx, end_t, 0)


def on_device(nbx, nby, *args):
    sol, forward_x = args[0], args[7]
    planes, rows, lanes = sol.shape
    nx, ny = forward_x.shape[1], rows * nby
    quarter = rows // 4
    wide = planes * lanes
    vmem = pl.BlockSpec(memory_space=pltpu.VMEM)
    far = pl.BlockSpec(memory_space=pltpu.HBM)
    dma = pltpu.SemaphoreType.DMA
    near = [pltpu.VMEM] * 3 + [pltpu.SMEM] + [pltpu.VMEM] * 2 + [pltpu.SMEM]
    near += [None] * 2 + [pltpu.VMEM] + [None] * 2 + [pltpu.VMEM] * 3 + [pltpu.SMEM]
    return pl.pallas_call(
        functools.partial(kernel, nbx, nby),
        out_shape=jax.ShapeDtypeStruct(sol.shape, F32),
        in_specs=[far] * len(args),
        out_specs=vmem,
        scratch_shapes=[space(arg.shape, arg.dtype) for space, arg in zip(near, args) if space]
        + [
            dma((12,)),
            pltpu.VMEM((planes, rows, lanes), F32),
            pltpu.VMEM((planes, rows, lanes), F32),
            pltpu.VMEM((2, 2 * planes, lanes), F32),
            pltpu.VMEM((2, 2 * planes, lanes), F32),
            pltpu.VMEM((2, 2 * planes, lanes), F32),
            pltpu.VMEM((2, 2 * planes, lanes), F32),
            pltpu.VMEM((2, rows, ny), BF16),
            pltpu.VMEM((2, 2, rows, ny // 2), BF16),
            pltpu.VMEM((2, rows, ny // 2), BF16),
            pltpu.VMEM((2, 4, lanes, nx), BF16),
            pltpu.VMEM((4, 1, lanes), F32),
            pltpu.VMEM((2, ny // 2, wide), BF16),
            pltpu.VMEM((2, 2, rows, wide // 2), BF16),
            pltpu.VMEM((2, 2, rows, wide // 2), BF16),
            pltpu.VMEM((2, 4, planes * quarter, lanes), BF16),
            pltpu.VMEM((2, nbx, planes * quarter, lanes), BF16),
            pltpu.VMEM((nbx // 4, planes * quarter, 4 * lanes), BF16),
            pltpu.VMEM((4, quarter, wide), BF16),
            dma((4,)),
            dma((4,)),
            dma((4,)),
            dma((2,)),
            dma((2,)),
            dma((9,)),
            dma((9,)),
            dma((2, nby // 2 - 1, SUBS)),
            dma((2, nby // 2, SUBS)),
            dma((2, 2)),
            dma((2, 2)),
            dma((2 * nbx,)),
            dma((2 * nbx,)),
            dma((nbx // 4,)),
            dma((nbx // 4,)),
            dma((4,)),
            dma((4,)),
        ],
        compiler_params=pltpu.CompilerParams(
            collective_id=0, has_side_effects=True, vmem_limit_bytes=60 << 20
        ),
    )(*args)


def solution(mesh):
    nbx, nby = mesh.shape["bx"], mesh.shape["by"]
    brick = P(None, "by", "bx")
    placed = (
        brick, brick, brick, P(), P("bx"), P("by"), P(), P("bx", None), P("by", None), P(),
        P("bx", None), P("by", None), P(), P("bx"), P("by"), P(),
    )
    return jax.shard_map(
        functools.partial(on_device, nbx, nby),
        mesh=mesh,
        in_specs=placed,
        out_specs=brick,
        check_vma=False,
    )
```

```python
import functools

import jax
import jax.numpy as jnp
from jax import lax
from jax.experimental import pallas as pl
from jax.experimental.pallas import tpu as pltpu
from jax.sharding import PartitionSpec as P

CLASSES = 8
SHIFT = 0.1
SUBS = 2
MESH = pl.DeviceIdType.MESH
F32 = jnp.float32
BF16 = jnp.bfloat16


def dot(a, b):
    return lax.dot_general(a, b, (((1,), (0,)), ((), ())), preferred_element_type=F32)


def dot_t(a, b):
    return lax.dot_general(a, b, (((1,), (1,)), ((), ())), preferred_element_type=F32)


def iota(shape, dim):
    return lax.broadcasted_iota(jnp.int32, shape, dim)


def to_row(column, width):
    size = column.shape[0]
    spread = jnp.where(iota((size, width), 0) == iota((size, width), 1), column, 0.0)
    return jnp.sum(spread, axis=0, keepdims=True)


def to_column(row, size):
    width = row.shape[1]
    spread = jnp.where(iota((size, width), 0) == iota((size, width), 1), row, 0.0)
    return jnp.sum(spread, axis=1, keepdims=True)


def face(c, cn):
    return jnp.where(cn > 0, 2.0 * c * cn / (c + cn), c)


def remote(src, dst, send, recv, bx, by):
    return pltpu.make_async_remote_copy(
        src_ref=src,
        dst_ref=dst,
        send_sem=send,
        recv_sem=recv,
        device_id={"bx": bx, "by": by},
        device_id_type=MESH,
    )


def kernel(
    nbx,
    nby,
    sol_far,
    src_far,
    cls_far,
    cond_far,
    sx_far,
    sy_far,
    sz_far,
    fx_ref,
    fy_ref,
    fz_far,
    ix_ref,
    iy_ref,
    iz_far,
    ex_far,
    ey_far,
    ez_far,
    out_ref,
    sol_ref,
    src_ref,
    cls_ref,
    cond_ref,
    sx_ref,
    sy_ref,
    sz_ref,
    fz_ref,
    iz_ref,
    ex_ref,
    ey_ref,
    ez_ref,
    small_sem,
    coef,
    acc,
    xmsg,
    ymsg,
    xhalo,
    yhalo,
    raw_y,
    keep_y,
    pass_y,
    all_x,
    all_ex,
    pencil0,
    pencil1,
    half_out,
    half_in,
    tsend,
    tall,
    sall,
    uside,
    halo_send,
    halo_recv,
    load_sem,
    wy_send,
    wy_recv,
    wx_send,
    wx_recv,
    ring_send,
    ring_recv,
    half_send,
    half_recv,
    t_send,
    t_recv,
    s_send,
    s_recv,
    u_send,
    u_recv,
):
    bx, by = lax.axis_index("bx"), lax.axis_index("by")
    nz, ny4 = nby // 2, nbx // 4
    z, xh = by // 2, by % 2
    xl, row4, core = bx // (2 * ny4), (bx // 2) % ny4, bx % 2
    mine4 = 2 * xl + core
    other = by + 1 - 2 * xh

    chips_x, cores = (xl, 1 - xl), (core, 1 - core)
    along_y = [2 * row4] + [2 * ((row4 + o) % ny4) for o in range(1, ny4)]
    starts_x = [value * (2 * ny4) for value in chips_x]
    sides_y = (by, other)

    def place(dx, dy, dc):
        return starts_x[dx] + along_y[dy] + cores[dc]

    def relative(j):
        dx, dc = j // 2, j % 2
        return place(dx, 0, dc), 2 * chips_x[dx] + cores[dc]

    plane_back = {b: (z - b + nz) % nz if b else z for b in (0, 2, -2, 4, -4, 6, -6)}
    by_ahead = {a: (by + 2 * a + nby) % nby for a in (1, -1, 2, -2, 3, -3)}
    by_next = ((by + nby - 1) % nby, (by + 1) % nby)
    bx_next = ((bx + nbx - 1) % nbx, (bx + 1) % nbx)

    planes, rows, lanes = sol_ref.shape
    sub = rows // SUBS
    quarter = rows // 4

    part_wide = planes * lanes // SUBS
    part_planes = planes // SUBS
    part_rows = part_planes * quarter
    barrier = pltpu.get_barrier_semaphore()

    def greet(to_bx, to_by):
        pl.semaphore_signal(
            barrier, inc=1, device_id={"bx": to_bx, "by": to_by}, device_id_type=MESH
        )

    near = (*by_next, *by_ahead.values())
    for to in near:
        greet(bx, to)
    layer = [
        (dx, dy, dc, cross)
        for cross in range(2)
        for dy in range(ny4)
        for dx in range(2)
        for dc in range(2)
    ]
    for dx, dy, dc, cross in layer:
        if dx or dy or dc:
            greet(place(dx, dy, dc), sides_y[cross])

    smalls = [
        pltpu.make_async_copy(far, ref, small_sem.at[n])
        for n, (far, ref) in enumerate(
            (
                (cls_far, cls_ref),
                (cond_far, cond_ref),
                (sol_far, sol_ref),
                (ex_far, ex_ref),
                (src_far, src_ref),
                (sx_far, sx_ref),
                (sy_far, sy_ref),
                (sz_far, sz_ref),
                (fz_far, fz_ref),
                (iz_far, iz_ref),
                (ey_far, ey_ref),
                (ez_far, ez_ref),
            )
        )
    ]
    for load in smalls:
        load.start()
    loads = [
        pltpu.make_async_copy(fy_ref, raw_y.at[0], load_sem.at[0]),
        pltpu.make_async_copy(iy_ref, raw_y.at[1], load_sem.at[1]),
        pltpu.make_async_copy(fx_ref, all_x.at[0, mine4], load_sem.at[2]),
        pltpu.make_async_copy(ix_ref, all_x.at[1, mine4], load_sem.at[3]),
    ]
    for load in loads:
        load.start()

    for load in smalls[:4]:
        load.wait()
    for k in range(planes):
        ids = cls_ref[k]
        value = jnp.zeros(ids.shape, F32)
        for index in range(CLASSES):
            value = jnp.where(ids == index, cond_ref[index], value)
        coef[k] = value
    for which, ref in enumerate((sol_ref, coef)):
        for k in range(planes):
            row = which * planes + k
            v = ref[k]
            xmsg[0, pl.ds(row, 1), :] = to_row(v[:, 0:1], lanes)
            xmsg[1, pl.ds(row, 1), :] = to_row(v[:, lanes - 1 : lanes], lanes)
            ymsg[0, pl.ds(row, 1), :] = v[0:1, :]
            ymsg[1, pl.ds(row, 1), :] = v[rows - 1 : rows, :]

    all_ex[pl.ds(mine4, 1)] = ex_ref[...].reshape(1, 1, lanes)
    pl.semaphore_wait(barrier, 2 * (nbx - 1) + len(near))

    halos = [
        remote(xmsg.at[0], xhalo.at[1], halo_send.at[0], halo_recv.at[0], bx_next[0], by),
        remote(xmsg.at[1], xhalo.at[0], halo_send.at[1], halo_recv.at[1], bx_next[1], by),
        remote(ymsg.at[0], yhalo.at[1], halo_send.at[2], halo_recv.at[2], bx, by_next[0]),
        remote(ymsg.at[1], yhalo.at[0], halo_send.at[3], halo_recv.at[3], bx, by_next[1]),
    ]
    for copy in halos:
        copy.start()

    shares_y = []
    low_lane = iota((rows, 128), 1) < 64
    for which in range(2):
        loads[which].wait()
        for pair in range(raw_y.shape[2] // 256):
            a = raw_y[which, :, 256 * pair : 256 * pair + 128].astype(F32)
            b = raw_y[which, :, 256 * pair + 128 : 256 * pair + 256].astype(F32)
            zero = jnp.where(low_lane, a, pltpu.roll(b, 64, 1))
            one = jnp.where(low_lane, pltpu.roll(a, 64, 1), b)
            where = slice(128 * pair, 128 * pair + 128)
            keep_y[which, pl.ds(xh, 1), :, where] = jnp.where(xh == 0, zero, one).astype(BF16)[None]
            pass_y[which, :, where] = jnp.where(xh == 0, one, zero).astype(BF16)
        copy = remote(
            pass_y.at[which], keep_y.at[which, xh], wy_send.at[which], wy_recv.at[which], bx, other
        )
        shares_y.append(copy)

    shares_x = []
    for which, ref in enumerate((fx_ref, ix_ref)):
        for j in (1, 2):
            at, number = all_x.at[which, mine4], 3 * which + j - 1
            shares_x.append(
                remote(ref, at, wx_send.at[number], wx_recv.at[number], relative(j)[0], by)
            )
    for j in (1, 2, 3):
        at, number = all_ex.at[mine4], 5 + j
        shares_x.append(remote(at, at, wx_send.at[number], wx_recv.at[number], relative(j)[0], by))
    for copy in (*shares_x[4:], shares_y[0], shares_x[1], shares_x[0]):
        copy.start()

    def pass_x(which):
        at, number = all_x.at[which, relative(2)[1]], 3 * which + 2
        return remote(at, at, wx_send.at[number], wx_recv.at[number], relative(1)[0], by)

    row_at, lane_at = iota((rows, lanes), 0), iota((rows, lanes), 1)
    for k in range(planes):
        u, c = sol_ref[k], coef[k]
        total = jnp.zeros((rows, lanes), F32)
        for n in (k + 1, k - 1):
            if 0 <= n < planes:
                total = total + face(c, coef[n]) * (u - sol_ref[n])
            else:
                total = total + c * u
        for dim, at, size in ((0, row_at, rows), (1, lane_at, lanes)):
            for shift, edge in ((1, 0), (size - 1, size - 1)):
                term = face(c, pltpu.roll(c, shift, dim)) * (u - pltpu.roll(u, shift, dim))
                total = total + jnp.where(at == edge, 0.0, term)
        acc[k] = total

    for load in smalls[4:]:
        load.wait()
    for copy in halos:
        copy.wait_recv()

    sides = (bx == 0, bx == nbx - 1, by == 0, by == nby - 1)
    ycol = to_column(sy_ref[...].reshape(1, rows), rows)
    area = ycol * sx_ref[...].reshape(1, lanes)
    for k in range(planes):
        u, c = sol_ref[k], coef[k]
        un, cn = [], []
        for side in range(2):
            halo = xhalo[side]
            gone = sides[side]
            un.append(jnp.where(gone, 0.0, to_column(halo[k : k + 1, :], rows)))
            cn.append(jnp.where(gone, 0.0, to_column(halo[planes + k : planes + k + 1, :], rows)))
        left = lane_at == 0
        term = face(c, jnp.where(left, cn[0], cn[1])) * (u - jnp.where(left, un[0], un[1]))
        total = acc[k] + jnp.where(left | (lane_at == lanes - 1), term, 0.0)
        for side, edge in ((0, 0), (1, rows - 1)):
            halo = yhalo[side]
            gone = sides[2 + side]
            un1 = jnp.where(gone, 0.0, halo[k : k + 1, :])
            cn1 = jnp.where(gone, 0.0, halo[planes + k : planes + k + 1, :])
            term = face(c, cn1) * (u - un1)
            total = total + jnp.where(row_at == edge, term, 0.0)
        value = (sz_ref[k] * area) * (src_ref[k] - total)
        at = pl.ds(pl.multiple_of(z * rows, rows), rows)
        at2 = (k % part_planes) * lanes
        pencil0[k // part_planes, at, at2 : at2 + lanes] = value.astype(BF16)

    ended = []

    def ring(phase, ready=None, done=None):
        def hop(number, behind, ahead, s):
            plane = plane_back[behind]
            if phase == 0:
                view = pencil0.at[s, pl.ds(pl.multiple_of(plane * rows, rows), rows)]
            else:
                part = (s + xl * (SUBS // 2)) % SUBS
                view = pencil1.at[pl.ds(pl.multiple_of(plane * rows + part * sub, sub), sub)]
            return remote(
                view,
                view,
                ring_send.at[phase, number, s],
                ring_recv.at[phase, (behind + ahead) % nz, s],
                bx,
                by_ahead[ahead],
            )

        def arrive(behind, s):
            view = pencil1.at[pl.ds(0, sub), :]
            send, recv = ring_send.at[phase, 0, s], ring_recv.at[phase, behind % nz, s]
            remote(view, view, send, recv, bx, other).wait_recv()

        parts = range(SUBS)
        for s in parts:
            if ready is not None:
                ready(s)
            for number, ahead in enumerate((2, -2)):
                hop(number, 0, ahead, s).start()
        for s in parts:
            for number, ahead in enumerate((1, -1)):
                hop(2 + number, 0, ahead, s).start()
        for stage, far in enumerate((2, 4)):
            for s in parts:
                for side, sign in enumerate((1, -1)):
                    arrive(far * sign, s)
                    for number, ahead in enumerate((2 * sign, sign)):
                        hop(4 + 4 * stage + 2 * side + number, far * sign, ahead, s).start()
        for s in parts:
            for side, sign in enumerate((1, -1)):
                arrive(6 * sign, s)
                hop(12 + side, 6 * sign, sign, s).start()
                if (s < SUBS // 2) == (side == 0):
                    hop(14, 6 * sign, 2 * sign, s).start()
        for s in parts:
            for behind in (1, 3, 5, 7):
                for sign in (1, -1):
                    arrive(behind * sign, s)
            arrive(8, s)
            if done is not None:
                done(s)

        for number in range(nz - 1):
            for s in parts:
                view = pencil1.at[pl.ds(0, sub), :]
                send, recv = ring_send.at[phase, number, s], ring_recv.at[phase, 0, s]
                ended.append(remote(view, view, send, recv, bx, other))

    def contract_y(phase):
        shares_y[phase].wait_recv()
        width = pencil1.shape[1] // 2
        mine, copies = [], []
        for piece in range(2):
            at = slice(piece * width, (piece + 1) * width)
            whole = pencil1[:, at]
            gone = dot(keep_y[phase, 1 - xh], whole)
            half_out[phase, piece] = gone.astype(BF16)
            copy = remote(
                half_out.at[phase, piece],
                half_in.at[phase, piece],
                half_send.at[phase, piece],
                half_recv.at[phase, piece],
                bx,
                other,
            )
            copy.start()
            copies.append(copy)
            mine.append(dot(keep_y[phase, xh], whole))
        for piece in range(2):
            copies[piece].wait_recv()
            mine[piece] = mine[piece] + half_in[phase, piece].astype(F32)
        for copy in copies:
            copy.wait_send()
        return [
            mine[k // (planes // 2)][:, (k % (planes // 2)) * lanes : (k % (planes // 2) + 1) * lanes]
            for k in range(planes)
        ]

    xh_of = (xh, 1 - xh)
    t_copies = []
    passed = [pass_x(0), pass_x(1)]

    def send_part(s):
        if s == 0:
            shares_y[0].wait_recv()
            shares_x[1].wait_recv()
            passed[0].start()
        sums = dot(keep_y[0].reshape(2 * rows, keep_y.shape[3]), pencil0[s]).astype(BF16)
        for side in range(2):
            for r in range(4):
                for k in range(part_planes):
                    row = side * rows + r * quarter
                    tsend[s, side, r, k * quarter : (k + 1) * quarter, :] = sums[
                        row : row + quarter, k * lanes : (k + 1) * lanes
                    ]
        for t, (dx, dy, dc, cross) in enumerate(layer):
            if t:
                copy = remote(
                    tsend.at[s, xh_of[cross], 2 * chips_x[dx] + cores[dc]],
                    tall.at[s, xh, bx],
                    t_send.at[t, s],
                    t_recv.at[((-dy) % ny4 * 4 + t % 4) + t // (4 * ny4) * (4 * ny4), s],
                    place(dx, dy, dc),
                    sides_y[cross],
                )
                copy.start()
                t_copies.append(copy)
        tall[s, pl.ds(xh, 1), pl.ds(bx, 1)] = tsend[s, pl.ds(xh, 1), pl.ds(mine4, 1)]

    ring(0, done=send_part)
    for copy in (shares_x[3], shares_x[2]):
        copy.start()

    def wait_t():
        for t in range(1, len(layer)):
            for s in range(SUBS):
                at = tall.at[0, 0, 0]
                remote(at, at, t_send.at[t, s], t_recv.at[t, s], bx, other).wait_recv()

    for load in loads[2:]:
        load.wait()
    for copy in (shares_x[0], shares_x[4], shares_x[5], shares_x[6], passed[0]):
        copy.wait_recv()
    wait_t()
    rows_x = jnp.concatenate(
        [
            jnp.concatenate([tall[s, side, n] for n in range(nbx)], axis=1)
            for side in range(2)
            for s in range(SUBS)
        ],
        axis=0,
    )
    both = dot_t(rows_x, all_x[0].reshape(4 * lanes, all_x.shape[3]))
    part_modes = both[: planes * quarter] + both[planes * quarter :]

    planes_xy = [part_modes[k * quarter : (k + 1) * quarter, :] for k in range(planes)]
    ey_all = to_column(ey_ref[...].reshape(1, rows), rows)
    ey = ey_all[:quarter]
    for r in range(1, 4):
        ey = jnp.where(mine4 == r, ey_all[r * quarter : (r + 1) * quarter], ey)
    ex = jnp.concatenate([all_ex[r] for r in range(4)], axis=1)
    fz, iz = fz_ref[...].astype(F32), iz_ref[...].astype(F32)
    scaled = []
    for q in range(planes):
        mode = sum(fz[q : q + 1, k : k + 1] * planes_xy[k] for k in range(planes))
        scaled.append(mode / (ex + ey + ez_ref[q] + SHIFT))
    for k in range(planes):
        value = sum(iz[k : k + 1, q : q + 1] * scaled[q] for q in range(planes))
        sall[pl.ds(row4, 1), k * quarter : (k + 1) * quarter, :] = value.astype(BF16)[None]

    s_copies = []
    for o in range(1, ny4):
        at = sall.at[row4]
        s_copies.append(remote(at, at, s_send.at[o], s_recv.at[o], place(0, o, 0), by))
    for copy in s_copies:
        copy.start()
    shares_x[3].wait_recv()
    passed[1].start()
    for copy in (shares_x[2], passed[1]):
        copy.wait_recv()
    for copy in s_copies:
        copy.wait_recv()
    rows_m = jnp.concatenate(
        [
            sall[n, :, (2 * side + c) * lanes : (2 * side + c + 1) * lanes]
            for side in range(2)
            for n in range(ny4)
            for c in range(2)
        ],
        axis=1,
    )
    cells_x = dot_t(rows_m, all_x[1].reshape(4 * lanes, all_x.shape[3])).astype(BF16)

    at = pl.ds(pl.multiple_of(z * rows + mine4 * quarter, quarter), quarter)
    for r in range(4):
        for k in range(planes):
            uside[r, :, k * lanes : (k + 1) * lanes] = cells_x[
                k * quarter : (k + 1) * quarter, r * lanes : (r + 1) * lanes
            ]
    u_copies = []
    for j in (2, 3, 1):
        to, r = relative(j)
        u_copies.append(
            remote(uside.at[r], pencil1.at[at, :], u_send.at[j], u_recv.at[j], to, by)
        )
    for copy in u_copies:
        copy.start()
    shares_y[1].start()
    pencil1[at, :] = uside[pl.ds(mine4, 1)].reshape(quarter, planes * lanes)

    def ready(s):
        for copy in u_copies[2:] if s == 0 else u_copies[:2]:
            copy.wait_recv()

    ring(1, ready)
    field = contract_y(1)
    for k in range(planes):
        out_ref[k] = sol_ref[k] + (sz_ref[k] * area) * field[k]

    for copy in halos + shares_x + shares_y + passed + s_copies + u_copies + t_copies + ended:
        copy.wait_send()


def on_device(nbx, nby, *args):
    sol, forward_x = args[0], args[7]
    planes, rows, lanes = sol.shape
    nx, ny = forward_x.shape[1], rows * nby
    quarter = rows // 4
    wide = planes * lanes
    vmem = pl.BlockSpec(memory_space=pltpu.VMEM)
    far = pl.BlockSpec(memory_space=pltpu.HBM)
    dma = pltpu.SemaphoreType.DMA
    near = [pltpu.VMEM] * 3 + [pltpu.SMEM] + [pltpu.VMEM] * 2 + [pltpu.SMEM]
    near += [None] * 2 + [pltpu.VMEM] + [None] * 2 + [pltpu.VMEM] * 3 + [pltpu.SMEM]
    return pl.pallas_call(
        functools.partial(kernel, nbx, nby),
        out_shape=jax.ShapeDtypeStruct(sol.shape, F32),
        in_specs=[far] * len(args),
        out_specs=vmem,
        scratch_shapes=[space(arg.shape, arg.dtype) for space, arg in zip(near, args) if space]
        + [
            dma((12,)),
            pltpu.VMEM((planes, rows, lanes), F32),
            pltpu.VMEM((planes, rows, lanes), F32),
            pltpu.VMEM((2, 2 * planes, lanes), F32),
            pltpu.VMEM((2, 2 * planes, lanes), F32),
            pltpu.VMEM((2, 2 * planes, lanes), F32),
            pltpu.VMEM((2, 2 * planes, lanes), F32),
            pltpu.VMEM((2, rows, ny), BF16),
            pltpu.VMEM((2, 2, rows, ny // 2), BF16),
            pltpu.VMEM((2, rows, ny // 2), BF16),
            pltpu.VMEM((2, 4, lanes, nx), BF16),
            pltpu.VMEM((4, 1, lanes), F32),
            pltpu.VMEM((SUBS, ny // 2, wide // SUBS), BF16),
            pltpu.VMEM((ny // 2, wide), BF16),
            pltpu.VMEM((2, 2, rows, wide // 2), BF16),
            pltpu.VMEM((2, 2, rows, wide // 2), BF16),
            pltpu.VMEM((SUBS, 2, 4, planes * quarter // SUBS, lanes), BF16),
            pltpu.VMEM((SUBS, 2, nbx, planes * quarter // SUBS, lanes), BF16),
            pltpu.VMEM((nbx // 4, planes * quarter, 4 * lanes), BF16),
            pltpu.VMEM((4, quarter, wide), BF16),
            dma((4,)),
            dma((4,)),
            dma((4,)),
            dma((2,)),
            dma((2,)),
            dma((9,)),
            dma((9,)),
            dma((2, nby // 2 - 1, SUBS)),
            dma((2, nby // 2, SUBS)),
            dma((2, 2)),
            dma((2, 2)),
            dma((2 * nbx, SUBS)),
            dma((2 * nbx, SUBS)),
            dma((nbx // 4,)),
            dma((nbx // 4,)),
            dma((4,)),
            dma((4,)),
        ],
        compiler_params=pltpu.CompilerParams(
            collective_id=0, has_side_effects=True, vmem_limit_bytes=60 << 20
        ),
    )(*args)


def solution(mesh):
    nbx, nby = mesh.shape["bx"], mesh.shape["by"]
    brick = P(None, "by", "bx")
    placed = (
        brick, brick, brick, P(), P("bx"), P("by"), P(), P("bx", None), P("by", None), P(),
        P("bx", None), P("by", None), P(), P("bx"), P("by"), P(),
    )
    return jax.shard_map(
        functools.partial(on_device, nbx, nby),
        mesh=mesh,
        in_specs=placed,
        out_specs=brick,
        check_vma=False,
    )
```

```python
import functools

import jax
import jax.numpy as jnp
from jax import lax
from jax.experimental import pallas as pl
from jax.experimental.pallas import tpu as pltpu
from jax.sharding import PartitionSpec as P

CLASSES = 8
SHIFT = 0.1
SUBS = 2
MESH = pl.DeviceIdType.MESH
F32 = jnp.float32
BF16 = jnp.bfloat16


def dot(a, b):
    return lax.dot_general(a, b, (((1,), (0,)), ((), ())), preferred_element_type=F32)


def dot_t(a, b):
    return lax.dot_general(a, b, (((1,), (1,)), ((), ())), preferred_element_type=F32)


def iota(shape, dim):
    return lax.broadcasted_iota(jnp.int32, shape, dim)


def to_row(column, width):
    size = column.shape[0]
    spread = jnp.where(iota((size, width), 0) == iota((size, width), 1), column, 0.0)
    return jnp.sum(spread, axis=0, keepdims=True)


def to_column(row, size):
    width = row.shape[1]
    spread = jnp.where(iota((size, width), 0) == iota((size, width), 1), row, 0.0)
    return jnp.sum(spread, axis=1, keepdims=True)


def face(c, cn):
    return jnp.where(cn > 0, 2.0 * c * cn / (c + cn), c)


def remote(src, dst, send, recv, bx, by):
    return pltpu.make_async_remote_copy(
        src_ref=src,
        dst_ref=dst,
        send_sem=send,
        recv_sem=recv,
        device_id={"bx": bx, "by": by},
        device_id_type=MESH,
    )


def kernel(
    nbx,
    nby,
    sol_far,
    src_far,
    cls_far,
    cond_far,
    sx_far,
    sy_far,
    sz_far,
    fx_ref,
    fy_ref,
    fz_far,
    ix_ref,
    iy_ref,
    iz_far,
    ex_far,
    ey_far,
    ez_far,
    out_ref,
    sol_ref,
    src_ref,
    cls_ref,
    cond_ref,
    sx_ref,
    sy_ref,
    sz_ref,
    fz_ref,
    iz_ref,
    ex_ref,
    ey_ref,
    ez_ref,
    small_sem,
    coef,
    acc,
    xmsg,
    ymsg,
    xhalo,
    yhalo,
    raw_y,
    keep_y,
    pass_y,
    all_x,
    all_ex,
    pencil0,
    pencil1,
    half_out,
    half_in,
    tsend,
    tall,
    sall,
    uside,
    halo_send,
    halo_recv,
    load_sem,
    wy_send,
    wy_recv,
    wx_send,
    wx_recv,
    ring_send,
    ring_recv,
    half_send,
    half_recv,
    t_send,
    t_recv,
    s_send,
    s_recv,
    u_send,
    u_recv,
):
    bx, by = lax.axis_index("bx"), lax.axis_index("by")
    nz, ny4 = nby // 2, nbx // 4
    z, xh = by // 2, by % 2
    xl, row4, core = bx // (2 * ny4), (bx // 2) % ny4, bx % 2
    mine4 = 2 * xl + core
    other = by + 1 - 2 * xh

    chips_x, cores = (xl, 1 - xl), (core, 1 - core)
    along_y = [2 * row4] + [2 * ((row4 + o) % ny4) for o in range(1, ny4)]
    starts_x = [value * (2 * ny4) for value in chips_x]
    sides_y = (by, other)

    def place(dx, dy, dc):
        return starts_x[dx] + along_y[dy] + cores[dc]

    def relative(j):
        dx, dc = j // 2, j % 2
        return place(dx, 0, dc), 2 * chips_x[dx] + cores[dc]

    plane_back = {b: (z - b + nz) % nz if b else z for b in (0, 2, -2, 4, -4, 6, -6)}
    by_ahead = {a: (by + 2 * a + nby) % nby for a in (1, -1, 2, -2, 3, -3)}
    by_next = ((by + nby - 1) % nby, (by + 1) % nby)
    bx_next = ((bx + nbx - 1) % nbx, (bx + 1) % nbx)

    planes, rows, lanes = sol_ref.shape
    sub = rows // SUBS
    quarter = rows // 4

    part_wide = planes * lanes // SUBS
    part_planes = planes // SUBS
    part_rows = part_planes * quarter
    barrier = pltpu.get_barrier_semaphore()

    def greet(to_bx, to_by):
        pl.semaphore_signal(
            barrier, inc=1, device_id={"bx": to_bx, "by": to_by}, device_id_type=MESH
        )

    near = (*by_next, *by_ahead.values())
    for to in near:
        greet(bx, to)
    layer = [
        (dx, dy, dc, cross)
        for cross in range(2)
        for dy in range(ny4)
        for dx in range(2)
        for dc in range(2)
    ]
    for dx, dy, dc, cross in layer:
        if dx or dy or dc:
            greet(place(dx, dy, dc), sides_y[cross])

    smalls = [
        pltpu.make_async_copy(far, ref, small_sem.at[n])
        for n, (far, ref) in enumerate(
            (
                (cls_far, cls_ref),
                (cond_far, cond_ref),
                (sol_far, sol_ref),
                (ex_far, ex_ref),
                (src_far, src_ref),
                (sx_far, sx_ref),
                (sy_far, sy_ref),
                (sz_far, sz_ref),
                (fz_far, fz_ref),
                (iz_far, iz_ref),
                (ey_far, ey_ref),
                (ez_far, ez_ref),
            )
        )
    ]
    for load in smalls:
        load.start()
    loads = [
        pltpu.make_async_copy(fy_ref, raw_y.at[0], load_sem.at[0]),
        pltpu.make_async_copy(iy_ref, raw_y.at[1], load_sem.at[1]),
        pltpu.make_async_copy(fx_ref, all_x.at[0, mine4], load_sem.at[2]),
        pltpu.make_async_copy(ix_ref, all_x.at[1, mine4], load_sem.at[3]),
    ]
    for load in loads:
        load.start()

    for load in smalls[:4]:
        load.wait()
    for k in range(planes):
        ids = cls_ref[k]
        value = jnp.zeros(ids.shape, F32)
        for index in range(CLASSES):
            value = jnp.where(ids == index, cond_ref[index], value)
        coef[k] = value
    for which, ref in enumerate((sol_ref, coef)):
        for k in range(planes):
            row = which * planes + k
            v = ref[k]
            xmsg[0, pl.ds(row, 1), :] = to_row(v[:, 0:1], lanes)
            xmsg[1, pl.ds(row, 1), :] = to_row(v[:, lanes - 1 : lanes], lanes)
            ymsg[0, pl.ds(row, 1), :] = v[0:1, :]
            ymsg[1, pl.ds(row, 1), :] = v[rows - 1 : rows, :]

    all_ex[pl.ds(mine4, 1)] = ex_ref[...].reshape(1, 1, lanes)
    pl.semaphore_wait(barrier, 2 * (nbx - 1) + len(near))

    halos = [
        remote(xmsg.at[0], xhalo.at[1], halo_send.at[0], halo_recv.at[0], bx_next[0], by),
        remote(xmsg.at[1], xhalo.at[0], halo_send.at[1], halo_recv.at[1], bx_next[1], by),
        remote(ymsg.at[0], yhalo.at[1], halo_send.at[2], halo_recv.at[2], bx, by_next[0]),
        remote(ymsg.at[1], yhalo.at[0], halo_send.at[3], halo_recv.at[3], bx, by_next[1]),
    ]
    for copy in halos:
        copy.start()

    shares_y = []
    low_lane = iota((rows, 128), 1) < 64

    def compact(which):
        loads[which].wait()
        for pair in range(raw_y.shape[2] // 256):
            a = raw_y[which, :, 256 * pair : 256 * pair + 128].astype(F32)
            b = raw_y[which, :, 256 * pair + 128 : 256 * pair + 256].astype(F32)
            zero = jnp.where(low_lane, a, pltpu.roll(b, 64, 1))
            one = jnp.where(low_lane, pltpu.roll(a, 64, 1), b)
            where = slice(128 * pair, 128 * pair + 128)
            keep_y[which, pl.ds(xh, 1), :, where] = jnp.where(xh == 0, zero, one).astype(BF16)[None]
            pass_y[which, :, where] = jnp.where(xh == 0, one, zero).astype(BF16)
        copy = remote(
            pass_y.at[which], keep_y.at[which, xh], wy_send.at[which], wy_recv.at[which], bx, other
        )
        shares_y.append(copy)

    compact(0)

    shares_x = []
    for which, ref in enumerate((fx_ref, ix_ref)):
        for j in (1, 2):
            at, number = all_x.at[which, mine4], 3 * which + j - 1
            shares_x.append(
                remote(ref, at, wx_send.at[number], wx_recv.at[number], relative(j)[0], by)
            )
    for j in (1, 2, 3):
        at, number = all_ex.at[mine4], 5 + j
        shares_x.append(remote(at, at, wx_send.at[number], wx_recv.at[number], relative(j)[0], by))
    for copy in (*shares_x[4:], shares_y[0], shares_x[1], shares_x[0]):
        copy.start()

    def pass_x(which):
        at, number = all_x.at[which, relative(2)[1]], 3 * which + 2
        return remote(at, at, wx_send.at[number], wx_recv.at[number], relative(1)[0], by)

    row_at, lane_at = iota((rows, lanes), 0), iota((rows, lanes), 1)
    for k in range(planes):
        u, c = sol_ref[k], coef[k]
        total = jnp.zeros((rows, lanes), F32)
        for n in (k + 1, k - 1):
            if 0 <= n < planes:
                total = total + face(c, coef[n]) * (u - sol_ref[n])
            else:
                total = total + c * u
        for dim, at, size in ((0, row_at, rows), (1, lane_at, lanes)):
            for shift, edge in ((1, 0), (size - 1, size - 1)):
                term = face(c, pltpu.roll(c, shift, dim)) * (u - pltpu.roll(u, shift, dim))
                total = total + jnp.where(at == edge, 0.0, term)
        acc[k] = total

    for load in smalls[4:]:
        load.wait()
    for copy in halos:
        copy.wait_recv()

    sides = (bx == 0, bx == nbx - 1, by == 0, by == nby - 1)
    ycol = to_column(sy_ref[...].reshape(1, rows), rows)
    area = ycol * sx_ref[...].reshape(1, lanes)
    for k in range(planes):
        u, c = sol_ref[k], coef[k]
        un, cn = [], []
        for side in range(2):
            halo = xhalo[side]
            gone = sides[side]
            un.append(jnp.where(gone, 0.0, to_column(halo[k : k + 1, :], rows)))
            cn.append(jnp.where(gone, 0.0, to_column(halo[planes + k : planes + k + 1, :], rows)))
        left = lane_at == 0
        term = face(c, jnp.where(left, cn[0], cn[1])) * (u - jnp.where(left, un[0], un[1]))
        total = acc[k] + jnp.where(left | (lane_at == lanes - 1), term, 0.0)
        for side, edge in ((0, 0), (1, rows - 1)):
            halo = yhalo[side]
            gone = sides[2 + side]
            un1 = jnp.where(gone, 0.0, halo[k : k + 1, :])
            cn1 = jnp.where(gone, 0.0, halo[planes + k : planes + k + 1, :])
            term = face(c, cn1) * (u - un1)
            total = total + jnp.where(row_at == edge, term, 0.0)
        value = (sz_ref[k] * area) * (src_ref[k] - total)
        at = pl.ds(pl.multiple_of(z * rows, rows), rows)
        at2 = (k % part_planes) * lanes
        pencil0[k // part_planes, at, at2 : at2 + lanes] = value.astype(BF16)

    ended = []

    def ring(phase, ready=None, done=None):
        def hop(number, behind, ahead, s):
            plane = plane_back[behind]
            if phase == 0:
                view = pencil0.at[s, pl.ds(pl.multiple_of(plane * rows, rows), rows)]
            else:
                part = (s + xl * (SUBS // 2)) % SUBS
                view = pencil1.at[pl.ds(pl.multiple_of(plane * rows + part * sub, sub), sub)]
            return remote(
                view,
                view,
                ring_send.at[phase, number, s],
                ring_recv.at[phase, (behind + ahead) % nz, s],
                bx,
                by_ahead[ahead],
            )

        def arrive(behind, s):
            view = pencil1.at[pl.ds(0, sub), :]
            send, recv = ring_send.at[phase, 0, s], ring_recv.at[phase, behind % nz, s]
            remote(view, view, send, recv, bx, other).wait_recv()

        parts = range(SUBS)
        for s in parts:
            if ready is not None:
                ready(s)
            for number, ahead in enumerate((2, -2)):
                hop(number, 0, ahead, s).start()
        for s in parts:
            for number, ahead in enumerate((1, -1)):
                hop(2 + number, 0, ahead, s).start()
        for stage, far in enumerate((2, 4)):
            for s in parts:
                for side, sign in enumerate((1, -1)):
                    arrive(far * sign, s)
                    for number, ahead in enumerate((2 * sign, sign)):
                        hop(4 + 4 * stage + 2 * side + number, far * sign, ahead, s).start()
        for s in parts:
            for side, sign in enumerate((1, -1)):
                arrive(6 * sign, s)
                hop(12 + side, 6 * sign, sign, s).start()
                if (s < SUBS // 2) == (side == 0):
                    hop(14, 6 * sign, 2 * sign, s).start()
        for s in parts:
            for behind in (1, 3, 5, 7):
                for sign in (1, -1):
                    arrive(behind * sign, s)
            arrive(8, s)
            if done is not None:
                done(s)

        for number in range(nz - 1):
            for s in parts:
                view = pencil1.at[pl.ds(0, sub), :]
                send, recv = ring_send.at[phase, number, s], ring_recv.at[phase, 0, s]
                ended.append(remote(view, view, send, recv, bx, other))

    def contract_y(phase):
        shares_y[phase].wait_recv()
        width = pencil1.shape[1] // 2
        mine, copies = [], []
        for piece in range(2):
            at = slice(piece * width, (piece + 1) * width)
            whole = pencil1[:, at]
            gone = dot(keep_y[phase, 1 - xh], whole)
            half_out[phase, piece] = gone.astype(BF16)
            copy = remote(
                half_out.at[phase, piece],
                half_in.at[phase, piece],
                half_send.at[phase, piece],
                half_recv.at[phase, piece],
                bx,
                other,
            )
            copy.start()
            copies.append(copy)
            mine.append(dot(keep_y[phase, xh], whole))
        for piece in range(2):
            copies[piece].wait_recv()
            mine[piece] = mine[piece] + half_in[phase, piece].astype(F32)
        for copy in copies:
            copy.wait_send()
        return [
            mine[k // (planes // 2)][:, (k % (planes // 2)) * lanes : (k % (planes // 2) + 1) * lanes]
            for k in range(planes)
        ]

    xh_of = (xh, 1 - xh)
    t_copies = []
    passed = [pass_x(0), pass_x(1)]

    def send_part(s):
        if s == 0:
            shares_y[0].wait_recv()
            shares_x[1].wait_recv()
            passed[0].start()
        sums = dot(keep_y[0].reshape(2 * rows, keep_y.shape[3]), pencil0[s]).astype(BF16)
        for side in range(2):
            for r in range(4):
                for k in range(part_planes):
                    row = side * rows + r * quarter
                    tsend[s, side, r, k * quarter : (k + 1) * quarter, :] = sums[
                        row : row + quarter, k * lanes : (k + 1) * lanes
                    ]
        for t, (dx, dy, dc, cross) in enumerate(layer):
            if t:
                copy = remote(
                    tsend.at[s, xh_of[cross], 2 * chips_x[dx] + cores[dc]],
                    tall.at[s, xh, bx],
                    t_send.at[t, s],
                    t_recv.at[((-dy) % ny4 * 4 + t % 4) + t // (4 * ny4) * (4 * ny4), s],
                    place(dx, dy, dc),
                    sides_y[cross],
                )
                copy.start()
                t_copies.append(copy)
        tall[s, pl.ds(xh, 1), pl.ds(bx, 1)] = tsend[s, pl.ds(xh, 1), pl.ds(mine4, 1)]

    ring(0, done=send_part)
    for copy in (shares_x[3], shares_x[2]):
        copy.start()
    compact(1)

    def wait_t():
        for t in range(1, len(layer)):
            for s in range(SUBS):
                at = tall.at[0, 0, 0]
                remote(at, at, t_send.at[t, s], t_recv.at[t, s], bx, other).wait_recv()

    for load in loads[2:]:
        load.wait()
    for copy in (shares_x[0], shares_x[4], shares_x[5], shares_x[6], passed[0]):
        copy.wait_recv()
    wait_t()
    rows_x = jnp.concatenate(
        [
            jnp.concatenate([tall[s, side, n] for n in range(nbx)], axis=1)
            for side in range(2)
            for s in range(SUBS)
        ],
        axis=0,
    )
    both = dot_t(rows_x, all_x[0].reshape(4 * lanes, all_x.shape[3]))
    part_modes = both[: planes * quarter] + both[planes * quarter :]

    planes_xy = [part_modes[k * quarter : (k + 1) * quarter, :] for k in range(planes)]
    ey_all = to_column(ey_ref[...].reshape(1, rows), rows)
    ey = ey_all[:quarter]
    for r in range(1, 4):
        ey = jnp.where(mine4 == r, ey_all[r * quarter : (r + 1) * quarter], ey)
    ex = jnp.concatenate([all_ex[r] for r in range(4)], axis=1)
    fz, iz = fz_ref[...].astype(F32), iz_ref[...].astype(F32)
    scaled = []
    for q in range(planes):
        mode = sum(fz[q : q + 1, k : k + 1] * planes_xy[k] for k in range(planes))
        scaled.append(mode / (ex + ey + ez_ref[q] + SHIFT))
    for k in range(planes):
        value = sum(iz[k : k + 1, q : q + 1] * scaled[q] for q in range(planes))
        sall[pl.ds(row4, 1), k * quarter : (k + 1) * quarter, :] = value.astype(BF16)[None]

    s_copies = []
    for o in range(1, ny4):
        at = sall.at[row4]
        s_copies.append(remote(at, at, s_send.at[o], s_recv.at[o], place(0, o, 0), by))
    for copy in s_copies:
        copy.start()
    shares_x[3].wait_recv()
    passed[1].start()
    for copy in (shares_x[2], passed[1]):
        copy.wait_recv()
    for copy in s_copies:
        copy.wait_recv()
    rows_m = jnp.concatenate(
        [
            sall[n, :, (2 * side + c) * lanes : (2 * side + c + 1) * lanes]
            for side in range(2)
            for n in range(ny4)
            for c in range(2)
        ],
        axis=1,
    )
    cells_x = dot_t(rows_m, all_x[1].reshape(4 * lanes, all_x.shape[3])).astype(BF16)

    at = pl.ds(pl.multiple_of(z * rows + mine4 * quarter, quarter), quarter)
    for r in range(4):
        for k in range(planes):
            uside[r, :, k * lanes : (k + 1) * lanes] = cells_x[
                k * quarter : (k + 1) * quarter, r * lanes : (r + 1) * lanes
            ]
    u_copies = []
    for j in (2, 3, 1):
        to, r = relative(j)
        u_copies.append(
            remote(uside.at[r], pencil1.at[at, :], u_send.at[j], u_recv.at[j], to, by)
        )
    for copy in u_copies:
        copy.start()
    shares_y[1].start()
    pencil1[at, :] = uside[pl.ds(mine4, 1)].reshape(quarter, planes * lanes)

    def ready(s):
        for copy in u_copies[2:] if s == 0 else u_copies[:2]:
            copy.wait_recv()

    ring(1, ready)
    field = contract_y(1)
    for k in range(planes):
        out_ref[k] = sol_ref[k] + (sz_ref[k] * area) * field[k]

    for copy in halos + shares_x + shares_y + passed + s_copies + u_copies + t_copies + ended:
        copy.wait_send()


def on_device(nbx, nby, *args):
    sol, forward_x = args[0], args[7]
    planes, rows, lanes = sol.shape
    nx, ny = forward_x.shape[1], rows * nby
    quarter = rows // 4
    wide = planes * lanes
    vmem = pl.BlockSpec(memory_space=pltpu.VMEM)
    far = pl.BlockSpec(memory_space=pltpu.HBM)
    dma = pltpu.SemaphoreType.DMA
    near = [pltpu.VMEM] * 3 + [pltpu.SMEM] + [pltpu.VMEM] * 2 + [pltpu.SMEM]
    near += [None] * 2 + [pltpu.VMEM] + [None] * 2 + [pltpu.VMEM] * 3 + [pltpu.SMEM]
    return pl.pallas_call(
        functools.partial(kernel, nbx, nby),
        out_shape=jax.ShapeDtypeStruct(sol.shape, F32),
        in_specs=[far] * len(args),
        out_specs=vmem,
        scratch_shapes=[space(arg.shape, arg.dtype) for space, arg in zip(near, args) if space]
        + [
            dma((12,)),
            pltpu.VMEM((planes, rows, lanes), F32),
            pltpu.VMEM((planes, rows, lanes), F32),
            pltpu.VMEM((2, 2 * planes, lanes), F32),
            pltpu.VMEM((2, 2 * planes, lanes), F32),
            pltpu.VMEM((2, 2 * planes, lanes), F32),
            pltpu.VMEM((2, 2 * planes, lanes), F32),
            pltpu.VMEM((2, rows, ny), BF16),
            pltpu.VMEM((2, 2, rows, ny // 2), BF16),
            pltpu.VMEM((2, rows, ny // 2), BF16),
            pltpu.VMEM((2, 4, lanes, nx), BF16),
            pltpu.VMEM((4, 1, lanes), F32),
            pltpu.VMEM((SUBS, ny // 2, wide // SUBS), BF16),
            pltpu.VMEM((ny // 2, wide), BF16),
            pltpu.VMEM((2, 2, rows, wide // 2), BF16),
            pltpu.VMEM((2, 2, rows, wide // 2), BF16),
            pltpu.VMEM((SUBS, 2, 4, planes * quarter // SUBS, lanes), BF16),
            pltpu.VMEM((SUBS, 2, nbx, planes * quarter // SUBS, lanes), BF16),
            pltpu.VMEM((nbx // 4, planes * quarter, 4 * lanes), BF16),
            pltpu.VMEM((4, quarter, wide), BF16),
            dma((4,)),
            dma((4,)),
            dma((4,)),
            dma((2,)),
            dma((2,)),
            dma((9,)),
            dma((9,)),
            dma((2, nby // 2 - 1, SUBS)),
            dma((2, nby // 2, SUBS)),
            dma((2, 2)),
            dma((2, 2)),
            dma((2 * nbx, SUBS)),
            dma((2 * nbx, SUBS)),
            dma((nbx // 4,)),
            dma((nbx // 4,)),
            dma((4,)),
            dma((4,)),
        ],
        compiler_params=pltpu.CompilerParams(
            collective_id=0, has_side_effects=True, vmem_limit_bytes=60 << 20
        ),
    )(*args)


def solution(mesh):
    nbx, nby = mesh.shape["bx"], mesh.shape["by"]
    brick = P(None, "by", "bx")
    placed = (
        brick, brick, brick, P(), P("bx"), P("by"), P(), P("bx", None), P("by", None), P(),
        P("bx", None), P("by", None), P(), P("bx"), P("by"), P(),
    )
    return jax.shard_map(
        functools.partial(on_device, nbx, nby),
        mesh=mesh,
        in_specs=placed,
        out_specs=brick,
        check_vma=False,
    )
```

```python
import functools

import jax
import jax.numpy as jnp
from jax import lax
from jax.experimental import pallas as pl
from jax.experimental.pallas import tpu as pltpu
from jax.sharding import PartitionSpec as P

CLASSES = 8
SHIFT = 0.1
SUBS = 2
MESH = pl.DeviceIdType.MESH
F32 = jnp.float32
BF16 = jnp.bfloat16


def dot(a, b):
    return lax.dot_general(a, b, (((1,), (0,)), ((), ())), preferred_element_type=F32)


def dot_t(a, b):
    return lax.dot_general(a, b, (((1,), (1,)), ((), ())), preferred_element_type=F32)


def iota(shape, dim):
    return lax.broadcasted_iota(jnp.int32, shape, dim)


def to_row(column, width):
    size = column.shape[0]
    spread = jnp.where(iota((size, width), 0) == iota((size, width), 1), column, 0.0)
    return jnp.sum(spread, axis=0, keepdims=True)


def to_column(row, size):
    width = row.shape[1]
    spread = jnp.where(iota((size, width), 0) == iota((size, width), 1), row, 0.0)
    return jnp.sum(spread, axis=1, keepdims=True)


def face(c, cn):
    return jnp.where(cn > 0, 2.0 * c * cn / (c + cn), c)


def remote(src, dst, send, recv, bx, by):
    return pltpu.make_async_remote_copy(
        src_ref=src,
        dst_ref=dst,
        send_sem=send,
        recv_sem=recv,
        device_id={"bx": bx, "by": by},
        device_id_type=MESH,
    )


def kernel(
    nbx,
    nby,
    sol_far,
    src_far,
    cls_far,
    cond_far,
    sx_far,
    sy_far,
    sz_far,
    fx_ref,
    fy_ref,
    fz_far,
    ix_ref,
    iy_ref,
    iz_far,
    ex_far,
    ey_far,
    ez_far,
    out_ref,
    sol_ref,
    src_ref,
    cls_ref,
    cond_ref,
    sx_ref,
    sy_ref,
    sz_ref,
    fz_ref,
    iz_ref,
    ex_ref,
    ey_ref,
    ez_ref,
    small_sem,
    coef,
    acc,
    xmsg,
    ymsg,
    xhalo,
    yhalo,
    raw_y,
    keep_y,
    pass_y,
    all_x,
    all_ex,
    pencil0,
    pencil1,
    half_out,
    half_in,
    tsend,
    tall,
    sall,
    uside,
    halo_send,
    halo_recv,
    load_sem,
    wy_send,
    wy_recv,
    wx_send,
    wx_recv,
    ring_send,
    ring_recv,
    half_send,
    half_recv,
    t_send,
    t_recv,
    s_send,
    s_recv,
    u_send,
    u_recv,
):
    bx, by = lax.axis_index("bx"), lax.axis_index("by")
    nz, ny4 = nby // 2, nbx // 4
    z, xh = by // 2, by % 2
    xl, row4, core = bx // (2 * ny4), (bx // 2) % ny4, bx % 2
    mine4 = 2 * xl + core
    other = by + 1 - 2 * xh

    chips_x, cores = (xl, 1 - xl), (core, 1 - core)
    along_y = [2 * row4] + [2 * ((row4 + o) % ny4) for o in range(1, ny4)]
    starts_x = [value * (2 * ny4) for value in chips_x]
    sides_y = (by, other)

    def place(dx, dy, dc):
        return starts_x[dx] + along_y[dy] + cores[dc]

    def relative(j):
        dx, dc = j // 2, j % 2
        return place(dx, 0, dc), 2 * chips_x[dx] + cores[dc]

    plane_back = {b: (z - b + nz) % nz if b else z for b in (0, 2, -2, 4, -4, 6, -6)}
    by_ahead = {a: (by + 2 * a + nby) % nby for a in (1, -1, 2, -2, 3, -3)}
    by_next = ((by + nby - 1) % nby, (by + 1) % nby)
    bx_next = ((bx + nbx - 1) % nbx, (bx + 1) % nbx)

    planes, rows, lanes = sol_ref.shape
    sub = rows // SUBS
    quarter = rows // 4

    part_wide = planes * lanes // SUBS
    part_planes = planes // SUBS
    part_rows = part_planes * quarter
    barrier = pltpu.get_barrier_semaphore()

    def greet(to_bx, to_by):
        pl.semaphore_signal(
            barrier, inc=1, device_id={"bx": to_bx, "by": to_by}, device_id_type=MESH
        )

    near = (*by_next, *by_ahead.values())
    for to in near:
        greet(bx, to)
    layer = [
        (dx, dy, dc, cross)
        for cross in range(2)
        for dy in range(ny4)
        for dx in range(2)
        for dc in range(2)
    ]
    for dx, dy, dc, cross in layer:
        if dx or dy or dc:
            greet(place(dx, dy, dc), sides_y[cross])

    smalls = [
        pltpu.make_async_copy(far, ref, small_sem.at[n])
        for n, (far, ref) in enumerate(
            (
                (cls_far, cls_ref),
                (cond_far, cond_ref),
                (sol_far, sol_ref),
                (ex_far, ex_ref),
                (src_far, src_ref),
                (sx_far, sx_ref),
                (sy_far, sy_ref),
                (sz_far, sz_ref),
                (fz_far, fz_ref),
                (iz_far, iz_ref),
                (ey_far, ey_ref),
                (ez_far, ez_ref),
            )
        )
    ]
    for load in smalls:
        load.start()
    loads = [
        pltpu.make_async_copy(fy_ref, raw_y.at[0], load_sem.at[0]),
        pltpu.make_async_copy(iy_ref, raw_y.at[1], load_sem.at[1]),
        pltpu.make_async_copy(fx_ref, all_x.at[0, mine4], load_sem.at[2]),
        pltpu.make_async_copy(ix_ref, all_x.at[1, mine4], load_sem.at[3]),
    ]
    for load in loads:
        load.start()

    for load in smalls[:4]:
        load.wait()
    for k in range(planes):
        ids = cls_ref[k]
        value = jnp.zeros(ids.shape, F32)
        for index in range(CLASSES):
            value = jnp.where(ids == index, cond_ref[index], value)
        coef[k] = value
    for which, ref in enumerate((sol_ref, coef)):
        for k in range(planes):
            row = which * planes + k
            v = ref[k]
            xmsg[0, pl.ds(row, 1), :] = to_row(v[:, 0:1], lanes)
            xmsg[1, pl.ds(row, 1), :] = to_row(v[:, lanes - 1 : lanes], lanes)
            ymsg[0, pl.ds(row, 1), :] = v[0:1, :]
            ymsg[1, pl.ds(row, 1), :] = v[rows - 1 : rows, :]

    all_ex[pl.ds(mine4, 1)] = ex_ref[...].reshape(1, 1, lanes)
    pl.semaphore_wait(barrier, 2 * (nbx - 1) + len(near))

    halos = [
        remote(xmsg.at[0], xhalo.at[1], halo_send.at[0], halo_recv.at[0], bx_next[0], by),
        remote(xmsg.at[1], xhalo.at[0], halo_send.at[1], halo_recv.at[1], bx_next[1], by),
        remote(ymsg.at[0], yhalo.at[1], halo_send.at[2], halo_recv.at[2], bx, by_next[0]),
        remote(ymsg.at[1], yhalo.at[0], halo_send.at[3], halo_recv.at[3], bx, by_next[1]),
    ]
    for copy in halos:
        copy.start()

    shares_y = []
    low_lane = iota((rows, 128), 1) < 64

    def compact(which):
        loads[which].wait()
        for pair in range(raw_y.shape[2] // 256):
            a = raw_y[which, :, 256 * pair : 256 * pair + 128].astype(F32)
            b = raw_y[which, :, 256 * pair + 128 : 256 * pair + 256].astype(F32)
            zero = jnp.where(low_lane, a, pltpu.roll(b, 64, 1))
            one = jnp.where(low_lane, pltpu.roll(a, 64, 1), b)
            where = slice(128 * pair, 128 * pair + 128)
            keep_y[which, pl.ds(xh, 1), :, where] = jnp.where(xh == 0, zero, one).astype(BF16)[None]
            pass_y[which, :, where] = jnp.where(xh == 0, one, zero).astype(BF16)
        copy = remote(
            pass_y.at[which], keep_y.at[which, xh], wy_send.at[which], wy_recv.at[which], bx, other
        )
        shares_y.append(copy)

    compact(0)

    shares_x = []
    for which, ref in enumerate((fx_ref, ix_ref)):
        for j in (1, 2):
            at, number = all_x.at[which, mine4], 3 * which + j - 1
            shares_x.append(
                remote(ref, at, wx_send.at[number], wx_recv.at[number], relative(j)[0], by)
            )
    for j in (1, 2, 3):
        at, number = all_ex.at[mine4], 5 + j
        shares_x.append(remote(at, at, wx_send.at[number], wx_recv.at[number], relative(j)[0], by))
    for copy in (*shares_x[4:], shares_y[0], shares_x[1], shares_x[0]):
        copy.start()

    def pass_x(which):
        at, number = all_x.at[which, relative(2)[1]], 3 * which + 2
        return remote(at, at, wx_send.at[number], wx_recv.at[number], relative(1)[0], by)

    row_at, lane_at = iota((rows, lanes), 0), iota((rows, lanes), 1)
    for k in range(planes):
        u, c = sol_ref[k], coef[k]
        total = jnp.zeros((rows, lanes), F32)
        for n in (k + 1, k - 1):
            if 0 <= n < planes:
                total = total + face(c, coef[n]) * (u - sol_ref[n])
            else:
                total = total + c * u
        for dim, at, size in ((0, row_at, rows), (1, lane_at, lanes)):
            for shift, edge in ((1, 0), (size - 1, size - 1)):
                term = face(c, pltpu.roll(c, shift, dim)) * (u - pltpu.roll(u, shift, dim))
                total = total + jnp.where(at == edge, 0.0, term)
        acc[k] = total

    for load in smalls[4:]:
        load.wait()
    for copy in halos:
        copy.wait_recv()

    sides = (bx == 0, bx == nbx - 1, by == 0, by == nby - 1)
    ycol = to_column(sy_ref[...].reshape(1, rows), rows)
    area = ycol * sx_ref[...].reshape(1, lanes)
    for k in range(planes):
        u, c = sol_ref[k], coef[k]
        un, cn = [], []
        for side in range(2):
            halo = xhalo[side]
            gone = sides[side]
            un.append(jnp.where(gone, 0.0, to_column(halo[k : k + 1, :], rows)))
            cn.append(jnp.where(gone, 0.0, to_column(halo[planes + k : planes + k + 1, :], rows)))
        left = lane_at == 0
        term = face(c, jnp.where(left, cn[0], cn[1])) * (u - jnp.where(left, un[0], un[1]))
        total = acc[k] + jnp.where(left | (lane_at == lanes - 1), term, 0.0)
        for side, edge in ((0, 0), (1, rows - 1)):
            halo = yhalo[side]
            gone = sides[2 + side]
            un1 = jnp.where(gone, 0.0, halo[k : k + 1, :])
            cn1 = jnp.where(gone, 0.0, halo[planes + k : planes + k + 1, :])
            term = face(c, cn1) * (u - un1)
            total = total + jnp.where(row_at == edge, term, 0.0)
        value = (sz_ref[k] * area) * (src_ref[k] - total)
        at = pl.ds(pl.multiple_of(z * rows, rows), rows)
        at2 = (k % part_planes) * lanes
        pencil0[k // part_planes, at, at2 : at2 + lanes] = value.astype(BF16)

    ended = []

    def ring(phase, ready=None, done=None):
        def hop(number, behind, ahead, s):
            plane = plane_back[behind]
            if phase == 0:
                view = pencil0.at[s, pl.ds(pl.multiple_of(plane * rows, rows), rows)]
            else:
                part = (s + xl * (SUBS // 2)) % SUBS
                view = pencil1.at[pl.ds(pl.multiple_of(plane * rows + part * sub, sub), sub)]
            return remote(
                view,
                view,
                ring_send.at[phase, number, s],
                ring_recv.at[phase, (behind + ahead) % nz, s],
                bx,
                by_ahead[ahead],
            )

        def arrive(behind, s):
            view = pencil1.at[pl.ds(0, sub), :]
            send, recv = ring_send.at[phase, 0, s], ring_recv.at[phase, behind % nz, s]
            remote(view, view, send, recv, bx, other).wait_recv()

        parts = range(SUBS)
        for s in parts:
            if ready is not None:
                ready(s)
            for number, ahead in enumerate((2, -2)):
                hop(number, 0, ahead, s).start()
        for s in parts:
            for number, ahead in enumerate((1, -1)):
                hop(2 + number, 0, ahead, s).start()
        for stage, far in enumerate((2, 4)):
            for s in parts:
                for side, sign in enumerate((1, -1)):
                    arrive(far * sign, s)
                    for number, ahead in enumerate((2 * sign, sign)):
                        hop(4 + 4 * stage + 2 * side + number, far * sign, ahead, s).start()
        for s in parts:
            for side, sign in enumerate((1, -1)):
                arrive(6 * sign, s)
                hop(12 + side, 6 * sign, sign, s).start()
                if (s < SUBS // 2) == (side == 0):
                    hop(14, 6 * sign, 2 * sign, s).start()
        for s in parts:
            for behind in (1, 3, 5, 7):
                for sign in (1, -1):
                    arrive(behind * sign, s)
            arrive(8, s)
            if done is not None:
                done(s)

        for number in range(nz - 1):
            for s in parts:
                view = pencil1.at[pl.ds(0, sub), :]
                send, recv = ring_send.at[phase, number, s], ring_recv.at[phase, 0, s]
                ended.append(remote(view, view, send, recv, bx, other))

    def contract_y(phase):
        shares_y[phase].wait_recv()
        width = pencil1.shape[1] // 2
        mine, copies = [], []
        for piece in range(2):
            at = slice(piece * width, (piece + 1) * width)
            whole = pencil1[:, at]
            gone = dot(keep_y[phase, 1 - xh], whole)
            half_out[phase, piece] = gone.astype(BF16)
            copy = remote(
                half_out.at[phase, piece],
                half_in.at[phase, piece],
                half_send.at[phase, piece],
                half_recv.at[phase, piece],
                bx,
                other,
            )
            copy.start()
            copies.append(copy)
        for piece in range(2):
            at = slice(piece * width, (piece + 1) * width)
            mine.append(dot(keep_y[phase, xh], pencil1[:, at]))
        for piece in range(2):
            copies[piece].wait_recv()
            mine[piece] = mine[piece] + half_in[phase, piece].astype(F32)
        for copy in copies:
            copy.wait_send()
        return [
            mine[k // (planes // 2)][:, (k % (planes // 2)) * lanes : (k % (planes // 2) + 1) * lanes]
            for k in range(planes)
        ]

    xh_of = (xh, 1 - xh)
    t_copies = []
    passed = [pass_x(0), pass_x(1)]

    def send_part(s):
        if s == 0:
            shares_y[0].wait_recv()
            shares_x[1].wait_recv()
            passed[0].start()
        sums = dot(keep_y[0].reshape(2 * rows, keep_y.shape[3]), pencil0[s]).astype(BF16)
        for side in range(2):
            for r in range(4):
                for k in range(part_planes):
                    row = side * rows + r * quarter
                    tsend[s, side, r, k * quarter : (k + 1) * quarter, :] = sums[
                        row : row + quarter, k * lanes : (k + 1) * lanes
                    ]
        for t, (dx, dy, dc, cross) in enumerate(layer):
            if t:
                copy = remote(
                    tsend.at[s, xh_of[cross], 2 * chips_x[dx] + cores[dc]],
                    tall.at[s, xh, bx],
                    t_send.at[t, s],
                    t_recv.at[((-dy) % ny4 * 4 + t % 4) + t // (4 * ny4) * (4 * ny4), s],
                    place(dx, dy, dc),
                    sides_y[cross],
                )
                copy.start()
                t_copies.append(copy)
        tall[s, pl.ds(xh, 1), pl.ds(bx, 1)] = tsend[s, pl.ds(xh, 1), pl.ds(mine4, 1)]

    ring(0, done=send_part)
    for copy in (shares_x[3], shares_x[2]):
        copy.start()
    compact(1)

    def wait_t():
        for t in range(1, len(layer)):
            for s in range(SUBS):
                at = tall.at[0, 0, 0]
                remote(at, at, t_send.at[t, s], t_recv.at[t, s], bx, other).wait_recv()

    for load in loads[2:]:
        load.wait()
    for copy in (shares_x[0], shares_x[4], shares_x[5], shares_x[6], passed[0]):
        copy.wait_recv()
    wait_t()
    rows_x = jnp.concatenate(
        [
            jnp.concatenate([tall[s, side, n] for n in range(nbx)], axis=1)
            for side in range(2)
            for s in range(SUBS)
        ],
        axis=0,
    )
    both = dot_t(rows_x, all_x[0].reshape(4 * lanes, all_x.shape[3]))
    part_modes = both[: planes * quarter] + both[planes * quarter :]

    planes_xy = [part_modes[k * quarter : (k + 1) * quarter, :] for k in range(planes)]
    ey_all = to_column(ey_ref[...].reshape(1, rows), rows)
    ey = ey_all[:quarter]
    for r in range(1, 4):
        ey = jnp.where(mine4 == r, ey_all[r * quarter : (r + 1) * quarter], ey)
    ex = jnp.concatenate([all_ex[r] for r in range(4)], axis=1)
    fz, iz = fz_ref[...].astype(F32), iz_ref[...].astype(F32)
    scaled = []
    for q in range(planes):
        mode = sum(fz[q : q + 1, k : k + 1] * planes_xy[k] for k in range(planes))
        scaled.append(mode / (ex + ey + ez_ref[q] + SHIFT))
    for k in range(planes):
        value = sum(iz[k : k + 1, q : q + 1] * scaled[q] for q in range(planes))
        sall[pl.ds(row4, 1), k * quarter : (k + 1) * quarter, :] = value.astype(BF16)[None]

    s_copies = []
    for o in range(1, ny4):
        at = sall.at[row4]
        s_copies.append(remote(at, at, s_send.at[o], s_recv.at[o], place(0, o, 0), by))
    for copy in s_copies:
        copy.start()
    shares_x[3].wait_recv()
    passed[1].start()
    for copy in (shares_x[2], passed[1]):
        copy.wait_recv()
    for copy in s_copies:
        copy.wait_recv()
    rows_m = jnp.concatenate(
        [
            sall[n, :, (2 * side + c) * lanes : (2 * side + c + 1) * lanes]
            for side in range(2)
            for n in range(ny4)
            for c in range(2)
        ],
        axis=1,
    )
    cells_x = dot_t(rows_m, all_x[1].reshape(4 * lanes, all_x.shape[3])).astype(BF16)

    at = pl.ds(pl.multiple_of(z * rows + mine4 * quarter, quarter), quarter)
    for r in range(4):
        for k in range(planes):
            uside[r, :, k * lanes : (k + 1) * lanes] = cells_x[
                k * quarter : (k + 1) * quarter, r * lanes : (r + 1) * lanes
            ]
    u_copies = []
    for j in (2, 3, 1):
        to, r = relative(j)
        u_copies.append(
            remote(uside.at[r], pencil1.at[at, :], u_send.at[j], u_recv.at[j], to, by)
        )
    for copy in u_copies:
        copy.start()
    shares_y[1].start()
    pencil1[at, :] = uside[pl.ds(mine4, 1)].reshape(quarter, planes * lanes)

    def ready(s):
        for copy in u_copies[2:] if s == 0 else u_copies[:2]:
            copy.wait_recv()

    ring(1, ready)
    field = contract_y(1)
    for k in range(planes):
        out_ref[k] = sol_ref[k] + (sz_ref[k] * area) * field[k]

    for copy in halos + shares_x + shares_y + passed + s_copies + u_copies + t_copies + ended:
        copy.wait_send()


def on_device(nbx, nby, *args):
    sol, forward_x = args[0], args[7]
    planes, rows, lanes = sol.shape
    nx, ny = forward_x.shape[1], rows * nby
    quarter = rows // 4
    wide = planes * lanes
    vmem = pl.BlockSpec(memory_space=pltpu.VMEM)
    far = pl.BlockSpec(memory_space=pltpu.HBM)
    dma = pltpu.SemaphoreType.DMA
    near = [pltpu.VMEM] * 3 + [pltpu.SMEM] + [pltpu.VMEM] * 2 + [pltpu.SMEM]
    near += [None] * 2 + [pltpu.VMEM] + [None] * 2 + [pltpu.VMEM] * 3 + [pltpu.SMEM]
    return pl.pallas_call(
        functools.partial(kernel, nbx, nby),
        out_shape=jax.ShapeDtypeStruct(sol.shape, F32),
        in_specs=[far] * len(args),
        out_specs=vmem,
        scratch_shapes=[space(arg.shape, arg.dtype) for space, arg in zip(near, args) if space]
        + [
            dma((12,)),
            pltpu.VMEM((planes, rows, lanes), F32),
            pltpu.VMEM((planes, rows, lanes), F32),
            pltpu.VMEM((2, 2 * planes, lanes), F32),
            pltpu.VMEM((2, 2 * planes, lanes), F32),
            pltpu.VMEM((2, 2 * planes, lanes), F32),
            pltpu.VMEM((2, 2 * planes, lanes), F32),
            pltpu.VMEM((2, rows, ny), BF16),
            pltpu.VMEM((2, 2, rows, ny // 2), BF16),
            pltpu.VMEM((2, rows, ny // 2), BF16),
            pltpu.VMEM((2, 4, lanes, nx), BF16),
            pltpu.VMEM((4, 1, lanes), F32),
            pltpu.VMEM((SUBS, ny // 2, wide // SUBS), BF16),
            pltpu.VMEM((ny // 2, wide), BF16),
            pltpu.VMEM((2, 2, rows, wide // 2), BF16),
            pltpu.VMEM((2, 2, rows, wide // 2), BF16),
            pltpu.VMEM((SUBS, 2, 4, planes * quarter // SUBS, lanes), BF16),
            pltpu.VMEM((SUBS, 2, nbx, planes * quarter // SUBS, lanes), BF16),
            pltpu.VMEM((nbx // 4, planes * quarter, 4 * lanes), BF16),
            pltpu.VMEM((4, quarter, wide), BF16),
            dma((4,)),
            dma((4,)),
            dma((4,)),
            dma((2,)),
            dma((2,)),
            dma((9,)),
            dma((9,)),
            dma((2, nby // 2 - 1, SUBS)),
            dma((2, nby // 2, SUBS)),
            dma((2, 2)),
            dma((2, 2)),
            dma((2 * nbx, SUBS)),
            dma((2 * nbx, SUBS)),
            dma((nbx // 4,)),
            dma((nbx // 4,)),
            dma((4,)),
            dma((4,)),
        ],
        compiler_params=pltpu.CompilerParams(
            collective_id=0, has_side_effects=True, vmem_limit_bytes=60 << 20
        ),
    )(*args)


def solution(mesh):
    nbx, nby = mesh.shape["bx"], mesh.shape["by"]
    brick = P(None, "by", "bx")
    placed = (
        brick, brick, brick, P(), P("bx"), P("by"), P(), P("bx", None), P("by", None), P(),
        P("bx", None), P("by", None), P(), P("bx"), P("by"), P(),
    )
    return jax.shard_map(
        functools.partial(on_device, nbx, nby),
        mesh=mesh,
        in_specs=placed,
        out_specs=brick,
        check_vma=False,
    )
```
